32 devices in a mesh: gx: 4 (over z), gy: 4 (over y, core), gz: 2 (over x).
Axes of the slice: x: 2, y: 2, z: 4, core: 2. Of those that a mesh axis runs over, the one named last changes fastest.
Arguments:
- positions: float32 [4, 4, 2, 3, 32, 128], P('gx', 'gy', 'gz'), may hold values from 0 to 1
- velocities: float32 [4, 4, 2, 3, 32, 128], P('gx', 'gy', 'gz'), may hold values from -6 to 6
- strength: float32 [4, 4, 2, 32, 128], P('gx', 'gy', 'gz'), may hold values from 0.5 to 2
- tower_slots: int32 [4, 4, 2, 128], P('gx', 'gy', 'gz'), may hold values from 0 to 159
- plate_slots: int32 [4, 4, 2, 128], P('gx', 'gy', 'gz'), may hold values from 0 to 191
- pair_count: int32 [4, 4, 2], P('gx', 'gy', 'gz'), may hold values from 16 to 128, as said below
Outputs:
- new_positions: float32 [4, 4, 2, 3, 32, 128], P('gx', 'gy', 'gz')
- new_velocities: float32 [4, 4, 2, 3, 32, 128], P('gx', 'gy', 'gz')
The draws below stay inside these ranges and needn't reach their ends.
Inputs may be any that keep to these rules, and one draw needn't show every extreme that they name: `pair_count`: slots at or beyond a device's count are padding. Some device has all 128 slots in use.
All inputs are finite; a program needn't handle non-finite values.
Results may differ from the reference program's by a relative error of at most 0.0003.
Values sent between devices are 32-bit elements; how exact they have to be, the bound alone decides.
No kernel may reach another device: no remote copies, remote signals or barrier semaphores. Data moves between devices by JAX's collectives and lax.ppermute only.
A program may use at most 64 MiB of HBM per device.

```python
import math
import jax
import jax.numpy as jnp
from jax import lax

CL = 32
CSIZE = 128
PAIR_CAP = 128
N_GX = 4
N_GY = 4
N_GZ = 2


def draw_pair_count(key, part):
    first_key, second_key = jax.random.split(jax.random.fold_in(key, 11))
    halvings = jax.random.randint(first_key, (N_GX, N_GY, N_GZ), 0, 4)
    counts = jnp.right_shift(jnp.full((N_GX, N_GY, N_GZ), PAIR_CAP, jnp.int32), halvings.astype(jnp.int32))
    busiest = jax.random.randint(second_key, (), 0, N_GX * N_GY * N_GZ)
    counts = counts.reshape(-1).at[busiest].set(PAIR_CAP)
    return counts.reshape((N_GX, N_GY, N_GZ)).astype(jnp.int32)


def plant(values, rng, least, high):
    longest = values.shape.index(max(values.shape))
    spots = []
    for shift in (0, 1):
        where = [jax.random.randint(jax.random.fold_in(rng, axis), (), 0, length) for axis, length in enumerate(values.shape)]
        where[longest] = (where[longest] + shift) % values.shape[longest]
        spots.append(tuple(where))
    return values.at[spots[0]].set(least).at[spots[1]].set(high)


def level_of(stream_key, extent, pieces, low, top_value):
    loudness, own = 1.0, jax.random.fold_in(stream_key, 6)
    for dim, parts in pieces:
        steps = jnp.exp(jax.random.uniform(jax.random.fold_in(own, dim), (parts,), jnp.float32, low / len(pieces), top_value / len(pieces)))
        loudness = loudness * jnp.repeat(steps, extent[dim] // parts).reshape([-1 if axis == dim else 1 for axis in range(len(extent))])
    return loudness


def noise(key, extent, deviation, reach, cuts=(), held_as=jnp.bfloat16):
    loudness = level_of(key, extent, cuts, -0.22, 0.18) if cuts else 1.0
    values = jax.random.normal(key, extent, jnp.float32) * deviation * loudness
    return jnp.minimum(jnp.maximum(values, -reach), reach).astype(held_as)


def setup_inputs(seed: int = 0) -> dict:
    splits = jax.random.split(jax.random.key(seed), 7)
    return {
        "positions": jnp.clip(1.0 * jax.random.uniform(splits[0], (N_GX, N_GY, N_GZ, 3, CL, CSIZE), jnp.float32) ** level_of(splits[0], (N_GX, N_GY, N_GZ, 3, CL, CSIZE), ((0, 4), (1, 4), (2, 2)), -0.2, 0.2), 0.0, 1.0),
        "velocities": noise(splits[1], (N_GX, N_GY, N_GZ, 3, CL, CSIZE), 1.0, 6.0, ((0, 4), (1, 4), (2, 2)), jnp.float32),
        "strength": jnp.clip(jnp.exp(math.log(2.0) - 1.3862944 * jax.random.uniform(splits[2], (N_GX, N_GY, N_GZ, CL, CSIZE), jnp.float32) ** level_of(splits[2], (N_GX, N_GY, N_GZ, CL, CSIZE), ((0, 4), (1, 4), (2, 2)), -0.2, 0.2)), 0.5, 2.0),
        "tower_slots": plant(jax.random.randint(splits[3], (N_GX, N_GY, N_GZ, PAIR_CAP), 0, 5 * CL), jax.random.fold_in(splits[3], 1), 0, (5 * CL) - 1).astype(jnp.int32),
        "plate_slots": plant(jax.random.randint(splits[4], (N_GX, N_GY, N_GZ, PAIR_CAP), 0, 3 * N_GZ * CL), jax.random.fold_in(splits[4], 1), 0, (3 * N_GZ * CL) - 1).astype(jnp.int32),
        "pair_count": draw_pair_count(jax.random.fold_in(splits[6], 71), 0),
    }


time_step = 0.02
cutoff_sq = 4.0
repulsion = 4.0
pair_block = 16


def placed_tower(tower_pos, height_level):
    shifts = (jnp.arange(5, dtype=jnp.float32) - 2.0)[:, None, None]
    return jnp.stack([tower_pos[:, 0] + shifts, tower_pos[:, 1], tower_pos[:, 2] + height_level], axis=1)


def placed_plate(plate_pos):
    line_shift = jnp.arange(plate_pos.shape[0], dtype=jnp.float32)[:, None, None, None]
    height_shift = jnp.arange(plate_pos.shape[1], dtype=jnp.float32)[None, :, None, None]
    return jnp.stack([plate_pos[:, :, 0], plate_pos[:, :, 1] + line_shift, plate_pos[:, :, 2] + height_shift], axis=2)


def block_forces(accum, begin_at, tower_pos, tower_str, plate_pos, plate_str, tower_list, plate_list, pair_total):
    tower_force, plate_force = accum
    clusters = tower_pos.shape[2]
    tower_pick = lax.dynamic_slice_in_dim(tower_list, begin_at, pair_block)
    plate_pick = lax.dynamic_slice_in_dim(plate_list, begin_at, pair_block)
    tower_block = tower_pick // clusters
    tower_index = tower_pick % clusters
    plate_block = plate_pick // clusters
    plate_index = plate_pick % clusters
    tower_side = tower_pos[tower_block, :, tower_index, :]
    plate_side = plate_pos[plate_block, :, plate_index, :]
    tower_weight = tower_str[tower_block, tower_index]
    plate_weight = plate_str[plate_block, plate_index]
    live_mask = (begin_at + jnp.arange(pair_block, dtype=jnp.int32) < pair_total).astype(jnp.float32)
    separation = tower_side[:, :, :, None] - plate_side[:, :, None, :]
    dist_sq = jnp.sum(separation * separation, axis=1)
    softness = jnp.maximum(1.0 - dist_sq / cutoff_sq, 0.0)
    weight = repulsion * softness * softness * tower_weight[:, :, None] * plate_weight[:, None, :] * live_mask[:, None, None]
    pair_push = weight[:, None] * separation
    tower_force = tower_force.at[tower_block, :, tower_index, :].add(jnp.sum(pair_push, axis=3))
    plate_force = plate_force.at[plate_block, :, plate_index, :].add(-jnp.sum(pair_push, axis=2))
    return tower_force, plate_force


def total_force(coords, strength, tower_slots, plate_slots, pair_count):
    rows_total = coords.shape[0]
    lines_total = coords.shape[1]
    heights_total = coords.shape[2]

    def column(accum, column_id):
        row_index = column_id // lines_total
        line_index = column_id % lines_total
        tower_all = jnp.stack([coords[(row_index + offset) % rows_total, line_index] for offset in (-2, -1, 0, 1, 2)])
        tower_str_all = jnp.stack([strength[(row_index + offset) % rows_total, line_index] for offset in (-2, -1, 0, 1, 2)])
        plate_all = jnp.stack([coords[row_index, (line_index + offset) % lines_total] for offset in (0, 1, 2)])
        plate_str_all = jnp.stack([strength[row_index, (line_index + offset) % lines_total] for offset in (0, 1, 2)])
        plate_flat = placed_plate(plate_all).reshape((3 * heights_total,) + plate_all.shape[2:])
        plate_str_flat = plate_str_all.reshape((3 * heights_total,) + plate_str_all.shape[2:])

        def one_height(height_id):
            tower_here = placed_tower(tower_all[:, height_id], height_id.astype(jnp.float32))
            tower_str_here = tower_str_all[:, height_id]
            tower_list = tower_slots[row_index, line_index, height_id]
            plate_list = plate_slots[row_index, line_index, height_id]
            pair_total = pair_count[row_index, line_index, height_id]
            start_force = (jnp.zeros(tower_here.shape, jnp.float32), jnp.zeros(plate_flat.shape, jnp.float32))

            def advance(block_id, state):
                return block_forces(state, block_id * pair_block, tower_here, tower_str_here, plate_flat, plate_str_flat, tower_list, plate_list, pair_total)

            return lax.fori_loop(0, PAIR_CAP // pair_block, advance, start_force)

        tower_force, plate_force = lax.map(one_height, jnp.arange(heights_total, dtype=jnp.int32))
        plate_sum = jnp.sum(plate_force, axis=0).reshape((3, heights_total) + plate_all.shape[2:])
        for offset in (-2, -1, 0, 1, 2):
            accum = accum.at[(row_index + offset) % rows_total, line_index].add(tower_force[:, offset + 2])
        for offset in (0, 1, 2):
            accum = accum.at[row_index, (line_index + offset) % lines_total].add(plate_sum[offset])
        return accum, None

    result, unused = lax.scan(column, jnp.zeros(coords.shape, jnp.float32), jnp.arange(rows_total * lines_total, dtype=jnp.int32))
    return result


def reference(positions, velocities, strength, tower_slots, plate_slots, pair_count):
    coords = positions
    speeds = velocities
    for leap_index in range(2):
        force = total_force(coords, strength, tower_slots, plate_slots, pair_count)
        speeds = speeds + time_step * force
        coords = coords + time_step * speeds
    return coords, speeds
```

```python
import functools

import jax
import jax.numpy as jnp
from jax import lax
from jax.experimental import pallas as pl
from jax.experimental.pallas import tpu as pltpu
from jax.sharding import PartitionSpec as P

time_step = 0.02
repulsion = 4.0
reach = 2
lines = 3
group = 4


def split_high(value):
    high = value.astype(jnp.bfloat16)
    return high, value - high.astype(jnp.float32)


def pieces(value):
    high, rest = split_high(value)
    middle, rest = split_high(rest)
    return high.astype(jnp.float32), middle.astype(jnp.float32), rest


def tower_operand(place, row):
    norm = jnp.sum(jnp.where(row < 3, place * place, 0.0), axis=0, keepdims=True) * -0.25
    norm = jnp.broadcast_to(norm, place.shape)
    high, middle, unused = pieces(place)
    norm_high, norm_middle, norm_low = pieces(norm)
    lower = jnp.where(row == 3, norm_high, jnp.where(row == 7, norm_middle, high))
    fixed = jnp.where(row == 7, 0.0, 1.0)
    upper = jnp.where(row < 3, middle, jnp.where(row == 3, norm_low, fixed))
    return jnp.concatenate([lower, upper], axis=0).astype(jnp.bfloat16)


def plate_operand(place, row):
    norm = jnp.sum(jnp.where(row < 3, place * place, 0.0), axis=0, keepdims=True)
    norm = jnp.broadcast_to(1.0 - 0.25 * norm, place.shape)
    high, middle, unused = pieces(0.5 * place)
    norm_high, norm_middle, norm_low = pieces(norm)
    lower = jnp.where((row == 3) | (row == 7), 1.0, jnp.where(row < 4, high, middle))
    tail = jnp.where(row == 4, norm_high, jnp.where(row == 5, norm_middle, norm_low))
    upper = jnp.where(row < 3, high, jnp.where(row == 3, 1.0, tail))
    return jnp.concatenate([lower, upper], axis=0).astype(jnp.bfloat16)


def charge_operand(place, strength, row):
    charge = jnp.where((row == 3) | (row == 7), 1.0, place) * strength
    high, middle, low = pieces(charge)
    lower = jnp.where(row < 4, high, middle)
    upper = jnp.where(row < 4, low, 0.0)
    return jnp.concatenate([lower, upper], axis=0).astype(jnp.bfloat16)


def push(total, place, scale):
    summed = total[0:8] + total[8:16]
    summed = summed[0:4] + summed[4:8]
    weight = summed[3:4]
    return scale * (place[0:3] * weight - summed[0:3])


def pair_kernel(
    height_ref,
    count_ref,
    tower_list,
    plate_list,
    tower_pos,
    tower_str,
    plate_pos,
    plate_str,
    tower_force,
    plate_force,
    *,
    clusters,
    rows_held,
    lines_held,
    heights,
):
    tower_force[...] = jnp.zeros_like(tower_force)
    plate_force[...] = jnp.zeros_like(plate_force)
    count = count_ref[0]
    height = height_ref[0]
    row = lax.broadcasted_iota(jnp.int32, (8, 128), 0)
    axis_of = row % 4

    def twice(value):
        return jnp.concatenate([value, value[0:1], value, value[0:1]], axis=0)

    def one(slot):
        live = jnp.where(slot < count, repulsion, 0.0)
        tower_slot = tower_list[slot]
        plate_slot = plate_list[slot]
        tower_block = tower_slot // clusters
        tower_index = tower_slot % clusters
        plate_block = plate_slot // clusters
        plate_index = plate_slot % clusters
        line = plate_block // heights
        level = plate_block % heights
        tower_held = lax.rem(tower_block, rows_held)
        rise = lax.rem(level - height + heights, heights)
        plate_held = lax.rem(line, lines_held) * heights + rise
        tower_base = tower_held * (3 * clusters) + tower_index
        plate_base = plate_held * (3 * clusters) + plate_index
        place_a = twice(tower_pos[pl.ds(tower_base, 3, stride=clusters), :]) - 0.5
        away = jnp.where(
            axis_of == 0,
            (reach - tower_block).astype(jnp.float32) - 0.5,
            jnp.where(
                axis_of == 1,
                line.astype(jnp.float32) - 0.5,
                (level - height).astype(jnp.float32) - 0.5,
            ),
        )
        place_q = twice(plate_pos[pl.ds(plate_base, 3, stride=clusters), :]) + away
        strength_a = tower_str[pl.ds(tower_held * clusters + tower_index, 1), :]
        strength_q = plate_str[pl.ds(plate_held * clusters + plate_index, 1), :]
        return place_a, place_q, strength_a, strength_q, live, tower_base, plate_base

    def advance(step, unused):
        begin = step * group
        made = [one(begin + member) for member in range(group)]
        softs = []
        for first in range(0, group, 2):
            left = jnp.concatenate(
                [tower_operand(made[first + side][0], row) for side in range(2)], axis=0
            )
            rights = [plate_operand(made[first + side][1], row) for side in range(2)]
            blank = jnp.zeros_like(rights[0])
            right = jnp.concatenate(
                [
                    jnp.concatenate([rights[0], blank], axis=1),
                    jnp.concatenate([blank, rights[1]], axis=1),
                ],
                axis=0,
            )
            soft = lax.dot_general(
                left, right, (((0,), (0,)), ((), ())), preferred_element_type=jnp.float32
            )
            softs += [soft[:, :128], soft[:, 128:]]
        for member in range(group):
            place_a, place_q, strength_a, strength_q, live, tower_base, plate_base = made[member]
            soft = jnp.maximum(softs[member], 0.0)
            high, rest = split_high(soft * soft)
            low = rest.astype(jnp.bfloat16)
            charge_a = charge_operand(place_a, strength_a, row)
            charge_q = charge_operand(place_q, strength_q, row)
            on_plate = jnp.dot(
                jnp.concatenate([charge_a, charge_a], axis=1),
                jnp.concatenate([high, low], axis=0),
                preferred_element_type=jnp.float32,
            )
            on_tower = lax.dot_general(
                jnp.concatenate([charge_q, charge_q], axis=1),
                jnp.concatenate([high, low], axis=1),
                (((1,), (1,)), ((), ())),
                preferred_element_type=jnp.float32,
            )
            tower_rows = pl.ds(tower_base, 3, stride=clusters)
            plate_rows = pl.ds(plate_base, 3, stride=clusters)
            tower_force[tower_rows, :] = tower_force[tower_rows, :] + push(
                on_tower, place_a, live * strength_a
            )
            plate_force[plate_rows, :] = plate_force[plate_rows, :] + push(
                on_plate, place_q, live * strength_q
            )
        return unused

    lax.fori_loop(0, (count + group - 1) // group, advance, 0)


def pair_forces(height, count, tower_list, plate_list, tower, plate, lines_held, heights):
    tower_pos, tower_str = tower
    plate_pos, plate_str = plate
    rows_held, unused, clusters, size = tower_pos.shape
    plates_held = plate_pos.shape[0]
    kernel = functools.partial(
        pair_kernel,
        clusters=clusters,
        rows_held=rows_held,
        lines_held=lines_held,
        heights=heights,
    )
    smem = pl.BlockSpec(memory_space=pltpu.SMEM)
    vmem = pl.BlockSpec(memory_space=pltpu.VMEM)
    pairs = tower_list.shape[0]
    tower_force, plate_force = pl.pallas_call(
        kernel,
        out_shape=(
            jax.ShapeDtypeStruct((rows_held * 3 * clusters, size), jnp.float32),
            jax.ShapeDtypeStruct((plates_held * 3 * clusters, size), jnp.float32),
        ),
        in_specs=[smem] * 4 + [vmem] * 4,
        out_specs=(vmem, vmem),
        cost_estimate=pl.CostEstimate(
            flops=pairs * size * size * 40, bytes_accessed=1 << 20, transcendentals=0
        ),
    )(
        height,
        count,
        tower_list,
        plate_list,
        tower_pos.reshape(-1, size),
        tower_str.reshape(-1, size),
        plate_pos.reshape(-1, size),
        plate_str.reshape(-1, size),
    )
    return (
        tower_force.reshape(tower_pos.shape),
        plate_force.reshape(plate_pos.shape),
    )


def shift_row(value, steps, count):
    return lax.ppermute(value, "gx", [(at, (at + steps) % count) for at in range(count)])


def shift_plane(value, line_steps, height_steps, line_count, height_count):
    pairs = [
        (
            at * height_count + up,
            (at + line_steps) % line_count * height_count + (up + height_steps) % height_count,
        )
        for at in range(line_count)
        for up in range(height_count)
    ]
    return lax.ppermute(value, ("gy", "gz"), pairs)


def plan(row_count, line_count, height_count):
    rows_held = min(row_count, 2 * reach + 1)
    lines_held = min(line_count, lines)
    rows = [(held - reach) % row_count for held in range(rows_held)]
    plates = [(line, rise) for line in range(lines_held) for rise in range(height_count)]
    return rows, plates, lines_held


def collect(value, rows, plates, sizes):
    row_count, line_count, height_count = sizes
    got_plates = {
        (line, rise): shift_plane(value, -line, -rise, line_count, height_count)
        for line, rise in plates
        if (line, rise) != (0, 0)
    }
    got_rows = {}
    for offset in sorted(rows, key=lambda at: min(at, row_count - at)):
        got_rows[offset] = value if offset == 0 else shift_row(value, -offset, row_count)
    got_plates[(0, 0)] = value
    return (
        jnp.stack([got_rows[offset] for offset in rows]),
        jnp.stack([got_plates[place] for place in plates]),
    )


def give_back(tower_force, plate_force, rows, plates, sizes):
    row_count, line_count, height_count = sizes
    total = tower_force[rows.index(0)] + plate_force[0]
    moved = []
    for at, (line, rise) in enumerate(plates):
        if (line, rise) != (0, 0):
            moved.append(shift_plane(plate_force[at], line, rise, line_count, height_count))
    for offset in sorted(rows, key=lambda at: min(at, row_count - at)):
        if offset != 0:
            moved.append(shift_row(tower_force[rows.index(offset)], offset, row_count))
    for part in moved:
        total = total + part
    return total


def shards(positions, velocities, strength, tower_slots, plate_slots, pair_count):
    coords = positions[0, 0, 0]
    speeds = velocities[0, 0, 0]
    tower_list = tower_slots[0, 0, 0]
    plate_list = plate_slots[0, 0, 0]
    count = pair_count.reshape(1)
    sizes = tuple(lax.axis_size(name) for name in ("gx", "gy", "gz"))
    rows, plates, lines_held = plan(*sizes)
    height = lax.axis_index("gz").astype(jnp.int32).reshape(1)
    strengths = None
    for leap_index in range(2):
        if strengths is None:
            packed = jnp.concatenate([coords, strength[0, 0]], axis=0)
            towers, plate_blocks = collect(packed, rows, plates, sizes)
            strengths = (towers[:, 3], plate_blocks[:, 3])
            towers = towers[:, :3]
            plate_blocks = plate_blocks[:, :3]
        else:
            towers, plate_blocks = collect(coords, rows, plates, sizes)
        tower_force, plate_force = pair_forces(
            height,
            count,
            tower_list,
            plate_list,
            (towers, strengths[0]),
            (plate_blocks, strengths[1]),
            lines_held,
            sizes[2],
        )
        force = give_back(tower_force, plate_force, rows, plates, sizes)
        speeds = speeds + time_step * force
        coords = coords + time_step * speeds
    return (coords[None, None, None], speeds[None, None, None])


def solution(mesh):
    in_specs = (
        P("gx", "gy", "gz", None, None, None),
        P("gx", "gy", "gz", None, None, None),
        P("gx", "gy", "gz", None, None),
        P("gx", "gy", "gz", None),
        P("gx", "gy", "gz", None),
        P("gx", "gy", "gz"),
    )
    out_specs = (P("gx", "gy", "gz", None, None, None), P("gx", "gy", "gz", None, None, None))
    return jax.shard_map(shards, mesh=mesh, in_specs=in_specs, out_specs=out_specs, check_vma=False)
```

```python
import functools

import jax
import jax.numpy as jnp
from jax import lax
from jax.experimental import pallas as pl
from jax.experimental.pallas import tpu as pltpu
from jax.sharding import PartitionSpec as P

time_step = 0.02
repulsion = 4.0
reach = 2
lines = 3
group = 16
planes = 24
grant = 24 << 20


def split(value):
    high = value.astype(jnp.bfloat16).astype(jnp.float32)
    return high, value - high


def split_three(value):
    high, rest = split(value)
    middle, low = split(rest)
    return high, middle, low


def norm_of(place):
    return place[0] * place[0] + place[1] * place[1] + place[2] * place[2]


def write_planes(planes, base, rows, clusters):
    for at, row in enumerate(rows):
        planes[pl.ds(base + at * clusters, clusters), :] = row


def charges(place, strength):
    parts = [split(strength * value) for value in place] + [split(strength)]
    return [part[0] for part in parts] + [part[1] for part in parts]


def tower_rows(place, strength):
    ones = jnp.ones_like(strength)
    parts = [split(value) for value in place]
    high = [part[0] for part in parts]
    middle = [part[1] for part in parts]
    norm = split_three(-0.25 * norm_of(place))
    operand = high + [norm[0]] + high + [norm[1]] + middle + [norm[2], ones, ones, ones, 0.0 * ones]
    return operand + charges(place, strength)


def plate_rows(place, strength):
    ones = jnp.ones_like(strength)
    parts = [split(0.5 * value) for value in place]
    high = [part[0] for part in parts]
    middle = [part[1] for part in parts]
    norm = split_three(1.0 - 0.25 * norm_of(place))
    operand = high + [ones] + middle + [ones] + high + [ones] + list(norm) + [0.0 * ones]
    return operand + charges(place, strength)


def apply_sums(sums, base, place, strength, clusters):
    row = [sums[pl.ds(base + at, clusters, stride=8), :] for at in range(8)]
    total = [row[at] + row[at + 4] for at in range(4)]
    scale = repulsion * strength
    return [scale * (place[at] * total[3] - total[at]) for at in range(3)]


def pair_kernel(*refs, rows_held, lines_held, heights, clusters):
    height_ref, count_ref, tower_list, plate_list = refs[:4]
    blocks = rows_held + lines_held * heights
    place_refs = refs[4 : 4 + blocks]
    strength_refs = refs[4 + blocks : 4 + 2 * blocks]
    force_refs = refs[4 + 2 * blocks : 4 + 3 * blocks - 1]
    tower_planes, plate_planes, tower_sums, plate_sums = refs[4 + 3 * blocks - 1 :]
    count = count_ref[0]
    height = height_ref[0]
    own_row = reach % rows_held
    towers = 2 * reach + 1

    def tower_place(block):
        ref = place_refs[block % rows_held]
        return [ref[0] + (block - reach - 0.5), ref[1] - 1.0, ref[2] - 0.5]

    def plate_slot(line, rise):
        level = height + rise
        level = jnp.where(level >= heights, level - heights, level)
        return line * heights + level, (level - height).astype(jnp.float32) - 0.5

    def plate_place(line, rise, above):
        ref = place_refs[rows_held + line % lines_held * heights + rise]
        return [ref[0] - 0.5, ref[1] + (line - 1.0), ref[2] + above]

    for block in range(towers):
        strength = strength_refs[block % rows_held][3]
        base = block * (planes * clusters)
        write_planes(tower_planes, base, tower_rows(tower_place(block), strength), clusters)
    for line in range(lines):
        for rise in range(heights):
            slot, above = plate_slot(line, rise)
            strength = strength_refs[rows_held + line % lines_held * heights + rise][3]
            base = pl.multiple_of(slot * (planes * clusters), planes * clusters)
            rows = plate_rows(plate_place(line, rise, above), strength)
            write_planes(plate_planes, base, rows, clusters)
    tower_sums[...] = jnp.zeros_like(tower_sums)
    plate_sums[...] = jnp.zeros_like(plate_sums)

    def operand_of(planes_ref, slot):
        base = lax.div(slot, clusters) * (planes * clusters) + lax.rem(slot, clusters)
        lower = planes_ref[pl.ds(base, 8, stride=clusters), :]
        upper = planes_ref[pl.ds(base + 8 * clusters, 8, stride=clusters), :]
        charge = planes_ref[pl.ds(base + 16 * clusters, 8, stride=clusters), :]
        return jnp.concatenate([lower, upper], axis=0).astype(jnp.bfloat16), charge

    def advance(step, unused):
        begin = step * group
        slots = [(tower_list[begin + at], plate_list[begin + at]) for at in range(group)]
        softs = []
        charged = []
        for first in range(0, group, 2):
            left = []
            right = []
            for side in range(2):
                tower_slot, plate_slot_at = slots[first + side]
                operand_a, charge_a = operand_of(tower_planes, tower_slot)
                operand_q, charge_q = operand_of(plate_planes, plate_slot_at)
                live = jnp.where(begin + first + side < count, 1.0, 0.0)
                charged.append((charge_a * live, charge_q * live))
                blank = jnp.zeros_like(operand_q)
                left.append(operand_a)
                pair = [operand_q, blank] if side == 0 else [blank, operand_q]
                right.append(jnp.concatenate(pair, axis=1))
            soft = lax.dot_general(
                jnp.concatenate(left, axis=0),
                jnp.concatenate(right, axis=0),
                (((0,), (0,)), ((), ())),
                preferred_element_type=jnp.float32,
            )
            softs += [soft[:, : soft.shape[1] // 2], soft[:, soft.shape[1] // 2 :]]
        results = []
        for at in range(group):
            soft = jnp.maximum(softs[at], 0.0)
            square = soft * soft
            high = square.astype(jnp.bfloat16)
            low = (square - high.astype(jnp.float32)).astype(jnp.bfloat16)
            charge_a = charged[at][0].astype(jnp.bfloat16)
            charge_q = charged[at][1].astype(jnp.bfloat16)
            on_plate = jnp.dot(
                jnp.concatenate([charge_a, charge_a], axis=1),
                jnp.concatenate([high, low], axis=0),
                preferred_element_type=jnp.float32,
            )
            on_tower = lax.dot_general(
                jnp.concatenate([charge_q, charge_q], axis=1),
                jnp.concatenate([high, low], axis=1),
                (((1,), (1,)), ((), ())),
                preferred_element_type=jnp.float32,
            )
            results.append((on_tower, on_plate))
        for at in range(group):
            tower_at = pl.ds(pl.multiple_of(slots[at][0] * 8, 8), 8)
            plate_at = pl.ds(pl.multiple_of(slots[at][1] * 8, 8), 8)
            tower_sums[tower_at, :] = tower_sums[tower_at, :] + results[at][0]
            plate_sums[plate_at, :] = plate_sums[plate_at, :] + results[at][1]
        return unused

    lax.fori_loop(0, lax.div(count + (group - 1), group), advance, 0)

    def tower_part(block):
        strength = strength_refs[block % rows_held][3]
        base = block * (8 * clusters)
        return apply_sums(tower_sums, base, tower_place(block), strength, clusters)

    def plate_part(line, rise):
        slot, above = plate_slot(line, rise)
        strength = strength_refs[rows_held + line % lines_held * heights + rise][3]
        base = pl.multiple_of(slot * (8 * clusters), 8 * clusters)
        return apply_sums(plate_sums, base, plate_place(line, rise, above), strength, clusters)

    def add(first, second):
        return [one + two for one, two in zip(first, second)]

    forces = {}
    for block in range(towers):
        place = block % rows_held
        part = tower_part(block)
        forces[place] = add(forces[place], part) if place in forces else part
    for line in range(lines):
        for rise in range(heights):
            place = rows_held + line % lines_held * heights + rise
            part = plate_part(line, rise)
            forces[place] = add(forces[place], part) if place in forces else part
    forces[own_row] = add(forces[own_row], forces.pop(rows_held))
    for ref, place in zip(force_refs, sorted(forces)):
        for at in range(3):
            ref[at] = forces[place][at]


def pair_forces(height, count, tower_list, plate_list, places, strengths, held, sizes):
    rows_held, lines_held = held
    heights = sizes[2]
    clusters, size = places[0].shape[1:]
    blocks = len(places)
    towers = 2 * reach + 1
    kernel = functools.partial(
        pair_kernel,
        rows_held=rows_held,
        lines_held=lines_held,
        heights=heights,
        clusters=clusters,
    )
    smem = pl.BlockSpec(memory_space=pltpu.SMEM)
    vmem = pl.BlockSpec(memory_space=pltpu.VMEM)
    pairs = tower_list.shape[0]
    force = jax.ShapeDtypeStruct((3, clusters, size), jnp.float32)
    return pl.pallas_call(
        kernel,
        out_shape=(force,) * (blocks - 1),
        in_specs=[smem] * 4 + [vmem] * (2 * blocks),
        out_specs=(vmem,) * (blocks - 1),
        scratch_shapes=[
            pltpu.VMEM((towers * planes * clusters, size), jnp.float32),
            pltpu.VMEM((lines * heights * planes * clusters, size), jnp.float32),
            pltpu.VMEM((towers * 8 * clusters, size), jnp.float32),
            pltpu.VMEM((lines * heights * 8 * clusters, size), jnp.float32),
        ],
        compiler_params=pltpu.CompilerParams(vmem_limit_bytes=grant),
        cost_estimate=pl.CostEstimate(
            flops=pairs * size * size * 40, bytes_accessed=1 << 20, transcendentals=0
        ),
    )(height, count, tower_list, plate_list, *places, *strengths)


def shift_row(value, steps, count):
    return lax.ppermute(value, "gx", [(at, (at + steps) % count) for at in range(count)])


def shift_plane(value, line_steps, height_steps, line_count, height_count):
    pairs = [
        (
            at * height_count + up,
            (at + line_steps) % line_count * height_count + (up + height_steps) % height_count,
        )
        for at in range(line_count)
        for up in range(height_count)
    ]
    return lax.ppermute(value, ("gy", "gz"), pairs)


def plan(row_count, line_count, height_count):
    rows_held = min(row_count, 2 * reach + 1)
    lines_held = min(line_count, lines)
    rows = [(held - reach) % row_count for held in range(rows_held)]
    plates = [(line, rise) for line in range(lines_held) for rise in range(height_count)]
    return rows, plates, lines_held


def collect(value, rows, plates, sizes):
    row_count, line_count, height_count = sizes
    got = {}
    for line, rise in plates:
        if (line, rise) != (0, 0):
            got[(line, rise)] = shift_plane(value, -line, -rise, line_count, height_count)
    for offset in sorted(rows, key=lambda at: min(at, row_count - at)):
        if offset != 0:
            got[offset] = shift_row(value, -offset, row_count)
    got[0] = got[(0, 0)] = value
    return [got[offset] for offset in rows] + [got[place] for place in plates]


def give_back(forces, rows, plates, sizes):
    row_count, line_count, height_count = sizes
    remote = dict(zip(list(rows) + [place for place in plates if place != (0, 0)], forces))
    total = remote.pop(0)
    moved = []
    for place, part in remote.items():
        if isinstance(place, tuple):
            moved.append(shift_plane(part, *place, line_count, height_count))
    for offset in sorted(rows, key=lambda at: min(at, row_count - at)):
        if offset != 0:
            moved.append(shift_row(remote[offset], offset, row_count))
    for part in moved:
        total = total + part
    return total


def shards(positions, velocities, strength, tower_slots, plate_slots, pair_count):
    coords = positions[0, 0, 0]
    speeds = velocities[0, 0, 0]
    tower_list = tower_slots[0, 0, 0]
    plate_list = plate_slots[0, 0, 0]
    count = pair_count.reshape(1)
    sizes = tuple(lax.axis_size(name) for name in ("gx", "gy", "gz"))
    rows, plates, lines_held = plan(*sizes)
    height = lax.axis_index("gz").astype(jnp.int32).reshape(1)
    packed = jnp.concatenate([coords, strength[0, 0]], axis=0)
    strengths = collect(packed, rows, plates, sizes)
    places = strengths
    for leap_index in range(2):
        if leap_index > 0:
            places = collect(coords, rows, plates, sizes)
        forces = pair_forces(
            height,
            count,
            tower_list,
            plate_list,
            places,
            strengths,
            (len(rows), lines_held),
            sizes,
        )
        force = give_back(forces, rows, plates, sizes)
        speeds = speeds + time_step * force
        coords = coords + time_step * speeds
    return (coords[None, None, None], speeds[None, None, None])


def solution(mesh):
    in_specs = (
        P("gx", "gy", "gz", None, None, None),
        P("gx", "gy", "gz", None, None, None),
        P("gx", "gy", "gz", None, None),
        P("gx", "gy", "gz", None),
        P("gx", "gy", "gz", None),
        P("gx", "gy", "gz"),
    )
    out_specs = (P("gx", "gy", "gz", None, None, None), P("gx", "gy", "gz", None, None, None))
    return jax.shard_map(shards, mesh=mesh, in_specs=in_specs, out_specs=out_specs, check_vma=False)
```

```python
import functools

import jax
import jax.numpy as jnp
from jax import lax
from jax.experimental import pallas as pl
from jax.experimental.pallas import tpu as pltpu
from jax.sharding import PartitionSpec as P

time_step = 0.02
repulsion = 4.0
reach = 2
lines = 3
group = 16
planes = 24
sums_pitch = 9
grant = 24 << 20


def split(value):
    high = value.astype(jnp.bfloat16).astype(jnp.float32)
    return high, value - high


def split_three(value):
    high, rest = split(value)
    middle, low = split(rest)
    return high, middle, low


def norm_of(place):
    return place[0] * place[0] + place[1] * place[1] + place[2] * place[2]


def write_planes(planes_ref, base, rows, clusters):
    for at, row in enumerate(rows):
        planes_ref[pl.ds(base + at * (clusters + 1), clusters), :] = row


def charges(place, strength):
    parts = [split(strength * value) for value in place] + [split(strength)]
    return [part[0] for part in parts] + [part[1] for part in parts]


def tower_rows(place, strength):
    ones = jnp.ones_like(strength)
    parts = [split(value) for value in place]
    high = [part[0] for part in parts]
    middle = [part[1] for part in parts]
    norm = split_three(-0.25 * norm_of(place))
    operand = high + [norm[0]] + high + [norm[1]] + middle + [norm[2], ones, ones, ones, 0.0 * ones]
    return operand + charges(place, strength)


def plate_rows(place, strength):
    ones = jnp.ones_like(strength)
    parts = [split(0.5 * value) for value in place]
    high = [part[0] for part in parts]
    middle = [part[1] for part in parts]
    norm = split_three(1.0 - 0.25 * norm_of(place))
    operand = high + [ones] + middle + [ones] + high + [ones] + list(norm) + [0.0 * ones]
    return operand + charges(place, strength)


def apply_sums(sums, base, place, strength, clusters):
    row = [sums[pl.ds(base + at, clusters, stride=sums_pitch), :] for at in range(8)]
    total = [row[at] + row[at + 4] for at in range(4)]
    scale = repulsion * strength
    return [scale * (place[at] * total[3] - total[at]) for at in range(3)]


def pair_kernel(*refs, rows_held, lines_held, heights, clusters):
    height_ref, count_ref, tower_list, plate_list = refs[:4]
    blocks = rows_held + lines_held * heights
    place_refs = refs[4 : 4 + blocks]
    strength_refs = refs[4 + blocks : 4 + 2 * blocks]
    force_refs = refs[4 + 2 * blocks : 4 + 3 * blocks - 1]
    tower_planes, plate_planes, tower_sums, plate_sums = refs[4 + 3 * blocks - 1 :]
    count = count_ref[0]
    height = height_ref[0]
    own_row = reach % rows_held
    towers = 2 * reach + 1
    pitch = clusters + 1

    def tower_place(block):
        ref = place_refs[block % rows_held]
        return [ref[0] + (block - reach - 0.5), ref[1] - 1.0, ref[2] - 0.5]

    def plate_slot(line, rise):
        level = height + rise
        level = jnp.where(level >= heights, level - heights, level)
        return line * heights + level, (level - height).astype(jnp.float32) - 0.5

    def plate_place(line, rise, above):
        ref = place_refs[rows_held + line % lines_held * heights + rise]
        return [ref[0] - 0.5, ref[1] + (line - 1.0), ref[2] + above]

    for block in range(towers):
        strength = strength_refs[block % rows_held][3]
        base = block * (planes * pitch)
        write_planes(tower_planes, base, tower_rows(tower_place(block), strength), clusters)
    for line in range(lines):
        for rise in range(heights):
            slot, above = plate_slot(line, rise)
            strength = strength_refs[rows_held + line % lines_held * heights + rise][3]
            base = slot * (planes * pitch)
            rows = plate_rows(plate_place(line, rise, above), strength)
            write_planes(plate_planes, base, rows, clusters)
    tower_sums[...] = jnp.zeros_like(tower_sums)
    plate_sums[...] = jnp.zeros_like(plate_sums)

    def operand_of(planes_ref, slot):
        base = lax.div(slot, clusters) * (planes * pitch) + lax.rem(slot, clusters)
        lower = planes_ref[pl.ds(base, 8, stride=pitch), :]
        upper = planes_ref[pl.ds(base + 8 * pitch, 8, stride=pitch), :]
        charge = planes_ref[pl.ds(base + 16 * pitch, 8, stride=pitch), :]
        return jnp.concatenate([lower, upper], axis=0).astype(jnp.bfloat16), charge

    def advance(step, unused):
        begin = step * group
        slots = [(tower_list[begin + at], plate_list[begin + at]) for at in range(group)]
        softs = []
        charged = []
        for first in range(0, group, 2):
            left = []
            right = []
            for side in range(2):
                tower_slot, plate_slot_at = slots[first + side]
                operand_a, charge_a = operand_of(tower_planes, tower_slot)
                operand_q, charge_q = operand_of(plate_planes, plate_slot_at)
                live = jnp.where(begin + first + side < count, 1.0, 0.0)
                charged.append((charge_a * live, charge_q * live))
                blank = jnp.zeros_like(operand_q)
                left.append(operand_a)
                pair = [operand_q, blank] if side == 0 else [blank, operand_q]
                right.append(jnp.concatenate(pair, axis=1))
            soft = lax.dot_general(
                jnp.concatenate(left, axis=0),
                jnp.concatenate(right, axis=0),
                (((0,), (0,)), ((), ())),
                preferred_element_type=jnp.float32,
            )
            softs += [soft[:, : soft.shape[1] // 2], soft[:, soft.shape[1] // 2 :]]
        results = []
        for at in range(group):
            soft = jnp.maximum(softs[at], 0.0)
            square = soft * soft
            high = square.astype(jnp.bfloat16)
            low = (square - high.astype(jnp.float32)).astype(jnp.bfloat16)
            charge_a = charged[at][0].astype(jnp.bfloat16)
            charge_q = charged[at][1].astype(jnp.bfloat16)
            on_plate = jnp.dot(
                jnp.concatenate([charge_a, charge_a], axis=1),
                jnp.concatenate([high, low], axis=0),
                preferred_element_type=jnp.float32,
            )
            on_tower = lax.dot_general(
                jnp.concatenate([charge_q, charge_q], axis=1),
                jnp.concatenate([high, low], axis=1),
                (((1,), (1,)), ((), ())),
                preferred_element_type=jnp.float32,
            )
            results.append((on_tower, on_plate))
        for at in range(group):
            tower_at = pl.ds(slots[at][0] * sums_pitch, 8)
            plate_at = pl.ds(slots[at][1] * sums_pitch, 8)
            tower_sums[tower_at, :] = tower_sums[tower_at, :] + results[at][0]
            plate_sums[plate_at, :] = plate_sums[plate_at, :] + results[at][1]
        return unused

    lax.fori_loop(0, lax.div(count + (group - 1), group), advance, 0)

    def tower_part(block):
        strength = strength_refs[block % rows_held][3]
        base = block * (sums_pitch * clusters)
        return apply_sums(tower_sums, base, tower_place(block), strength, clusters)

    def plate_part(line, rise):
        slot, above = plate_slot(line, rise)
        strength = strength_refs[rows_held + line % lines_held * heights + rise][3]
        base = slot * (sums_pitch * clusters)
        return apply_sums(plate_sums, base, plate_place(line, rise, above), strength, clusters)

    def add(first, second):
        return [one + two for one, two in zip(first, second)]

    forces = {}
    for block in range(towers):
        place = block % rows_held
        part = tower_part(block)
        forces[place] = add(forces[place], part) if place in forces else part
    for line in range(lines):
        for rise in range(heights):
            place = rows_held + line % lines_held * heights + rise
            part = plate_part(line, rise)
            forces[place] = add(forces[place], part) if place in forces else part
    forces[own_row] = add(forces[own_row], forces.pop(rows_held))
    for ref, place in zip(force_refs, sorted(forces)):
        for at in range(3):
            ref[at] = forces[place][at]


def pair_forces(height, count, tower_list, plate_list, places, strengths, held, sizes):
    rows_held, lines_held = held
    heights = sizes[2]
    clusters, size = places[0].shape[1:]
    blocks = len(places)
    towers = 2 * reach + 1
    kernel = functools.partial(
        pair_kernel,
        rows_held=rows_held,
        lines_held=lines_held,
        heights=heights,
        clusters=clusters,
    )
    smem = pl.BlockSpec(memory_space=pltpu.SMEM)
    vmem = pl.BlockSpec(memory_space=pltpu.VMEM)
    pairs = tower_list.shape[0]
    force = jax.ShapeDtypeStruct((3, clusters, size), jnp.float32)
    return pl.pallas_call(
        kernel,
        out_shape=(force,) * (blocks - 1),
        in_specs=[smem] * 4 + [vmem] * (2 * blocks),
        out_specs=(vmem,) * (blocks - 1),
        scratch_shapes=[
            pltpu.VMEM((towers * planes * (clusters + 1), size), jnp.float32),
            pltpu.VMEM((lines * heights * planes * (clusters + 1), size), jnp.float32),
            pltpu.VMEM((towers * sums_pitch * clusters, size), jnp.float32),
            pltpu.VMEM((lines * heights * sums_pitch * clusters, size), jnp.float32),
        ],
        compiler_params=pltpu.CompilerParams(vmem_limit_bytes=grant),
        cost_estimate=pl.CostEstimate(
            flops=pairs * size * size * 40, bytes_accessed=1 << 20, transcendentals=0
        ),
    )(height, count, tower_list, plate_list, *places, *strengths)


def shift_row(value, steps, count):
    return lax.ppermute(value, "gx", [(at, (at + steps) % count) for at in range(count)])


def shift_plane(value, line_steps, height_steps, line_count, height_count):
    pairs = [
        (
            at * height_count + up,
            (at + line_steps) % line_count * height_count + (up + height_steps) % height_count,
        )
        for at in range(line_count)
        for up in range(height_count)
    ]
    return lax.ppermute(value, ("gy", "gz"), pairs)


def plan(row_count, line_count, height_count):
    rows_held = min(row_count, 2 * reach + 1)
    lines_held = min(line_count, lines)
    rows = [(held - reach) % row_count for held in range(rows_held)]
    plates = [(line, rise) for line in range(lines_held) for rise in range(height_count)]
    return rows, plates, lines_held


def collect(value, rows, plates, sizes):
    row_count, line_count, height_count = sizes
    got = {}
    for line, rise in plates:
        if (line, rise) != (0, 0):
            got[(line, rise)] = shift_plane(value, -line, -rise, line_count, height_count)
    for offset in sorted(rows, key=lambda at: min(at, row_count - at)):
        if offset != 0:
            got[offset] = shift_row(value, -offset, row_count)
    got[0] = got[(0, 0)] = value
    return [got[offset] for offset in rows] + [got[place] for place in plates]


def give_back(forces, rows, plates, sizes):
    row_count, line_count, height_count = sizes
    remote = dict(zip(list(rows) + [place for place in plates if place != (0, 0)], forces))
    total = remote.pop(0)
    moved = []
    for place, part in remote.items():
        if isinstance(place, tuple):
            moved.append(shift_plane(part, *place, line_count, height_count))
    for offset in sorted(rows, key=lambda at: min(at, row_count - at)):
        if offset != 0:
            moved.append(shift_row(remote[offset], offset, row_count))
    for part in moved:
        total = total + part
    return total


def shards(positions, velocities, strength, tower_slots, plate_slots, pair_count):
    coords = positions[0, 0, 0]
    speeds = velocities[0, 0, 0]
    tower_list = tower_slots[0, 0, 0]
    plate_list = plate_slots[0, 0, 0]
    count = pair_count.reshape(1)
    sizes = tuple(lax.axis_size(name) for name in ("gx", "gy", "gz"))
    rows, plates, lines_held = plan(*sizes)
    height = lax.axis_index("gz").astype(jnp.int32).reshape(1)
    packed = jnp.concatenate([coords, strength[0, 0]], axis=0)
    strengths = collect(packed, rows, plates, sizes)
    places = strengths
    for leap_index in range(2):
        if leap_index > 0:
            places = collect(coords, rows, plates, sizes)
        forces = pair_forces(
            height,
            count,
            tower_list,
            plate_list,
            places,
            strengths,
            (len(rows), lines_held),
            sizes,
        )
        force = give_back(forces, rows, plates, sizes)
        speeds = speeds + time_step * force
        coords = coords + time_step * speeds
    return (coords[None, None, None], speeds[None, None, None])


def solution(mesh):
    in_specs = (
        P("gx", "gy", "gz", None, None, None),
        P("gx", "gy", "gz", None, None, None),
        P("gx", "gy", "gz", None, None),
        P("gx", "gy", "gz", None),
        P("gx", "gy", "gz", None),
        P("gx", "gy", "gz"),
    )
    out_specs = (P("gx", "gy", "gz", None, None, None), P("gx", "gy", "gz", None, None, None))
    return jax.shard_map(shards, mesh=mesh, in_specs=in_specs, out_specs=out_specs, check_vma=False)
```

```python
import functools

import jax
import jax.numpy as jnp
from jax import lax
from jax.experimental import pallas as pl
from jax.experimental.pallas import tpu as pltpu
from jax.sharding import PartitionSpec as P

time_step = 0.02
repulsion = 4.0
reach = 2
lines = 3
group = 8
planes = 24
grant = 32 << 20


def split(value):
    high = value.astype(jnp.bfloat16).astype(jnp.float32)
    return high, value - high


def split_three(value):
    high, rest = split(value)
    middle, low = split(rest)
    return high, middle, low


def norm_of(place):
    return place[0] * place[0] + place[1] * place[1] + place[2] * place[2]


def write_planes(planes_ref, base, rows, clusters):
    for at, row in enumerate(rows):
        planes_ref[pl.ds(base + at * (clusters + 1), clusters), :] = row


def charges(place, strength):
    parts = [split(strength * value) for value in place] + [split(strength)]
    return [part[0] for part in parts] + [part[1] for part in parts]


def tower_rows(place, strength):
    ones = jnp.ones_like(strength)
    parts = [split(value) for value in place]
    high = [part[0] for part in parts]
    middle = [part[1] for part in parts]
    norm = split_three(-0.25 * norm_of(place))
    operand = high + [norm[0]] + high + [norm[1]] + middle + [norm[2], ones, ones, ones, 0.0 * ones]
    return operand + charges(place, strength)


def plate_rows(place, strength):
    ones = jnp.ones_like(strength)
    parts = [split(0.5 * value) for value in place]
    high = [part[0] for part in parts]
    middle = [part[1] for part in parts]
    norm = split_three(1.0 - 0.25 * norm_of(place))
    operand = high + [ones] + middle + [ones] + high + [ones] + list(norm) + [0.0 * ones]
    return operand + charges(place, strength)


def apply_sums(sums, base, place, strength, clusters):
    row = [sums[pl.ds(base + at * (clusters + 1), clusters), :] for at in range(8)]
    total = [row[at] + row[at + 4] for at in range(4)]
    scale = repulsion * strength
    return [scale * (place[at] * total[3] - total[at]) for at in range(3)]


def pair_kernel(*refs, rows_held, lines_held, heights, clusters, order):
    height_ref, count_ref, tower_list, plate_list = refs[:4]
    blocks = rows_held + lines_held * heights
    place_refs = [refs[4 + order.index(block)] for block in range(blocks)]
    strength_refs = [refs[4 + blocks + order.index(block)] for block in range(blocks)]
    force_refs = refs[4 + 2 * blocks : 4 + 3 * blocks - 1]
    tower_planes, plate_planes, tower_sums, plate_sums, softs = refs[4 + 3 * blocks - 1 :]
    count = count_ref[0]
    height = height_ref[0]
    own_row = reach % rows_held
    towers = 2 * reach + 1
    pitch = clusters + 1
    blank_rows = jnp.zeros((8, tower_planes.shape[1]), jnp.float32)

    def tower_place(block):
        ref = place_refs[block % rows_held]
        return [ref[0] + (block - reach - 0.5), ref[1] - 1.0, ref[2] - 0.5]

    def plate_slot(line, rise):
        level = height + rise
        level = jnp.where(level >= heights, level - heights, level)
        return line * heights + level, (level - height).astype(jnp.float32) - 0.5

    def plate_place(line, rise, above):
        ref = place_refs[rows_held + line % lines_held * heights + rise]
        return [ref[0] - 0.5, ref[1] + (line - 1.0), ref[2] + above]

    for block in range(towers):
        strength = strength_refs[block % rows_held][3]
        base = block * (planes * pitch)
        write_planes(tower_planes, base, tower_rows(tower_place(block), strength), clusters)
    for line in range(lines):
        for rise in range(heights):
            slot, above = plate_slot(line, rise)
            strength = strength_refs[rows_held + line % lines_held * heights + rise][3]
            base = slot * (planes * pitch)
            rows = plate_rows(plate_place(line, rise, above), strength)
            write_planes(plate_planes, base, rows, clusters)
    for ref, sums, blocks_here in (
        (tower_planes, tower_sums, towers),
        (plate_planes, plate_sums, lines * heights),
    ):
        for at in range(0, planes, 8):
            ref[pl.ds(blocks_here * planes * pitch + at * pitch, 8, stride=pitch), :] = blank_rows
        for block in range(blocks_here + 1):
            sums[pl.ds(block * planes * pitch, 8 * pitch), :] = jnp.zeros(
                (8 * pitch, sums.shape[1]), jnp.float32
            )

    def operand_of(planes_ref, base):
        lower = planes_ref[pl.ds(base, 8, stride=pitch), :]
        upper = planes_ref[pl.ds(base + 8 * pitch, 8, stride=pitch), :]
        return jnp.concatenate([lower, upper], axis=0).astype(jnp.bfloat16)

    def charge_of(planes_ref, base):
        charge = planes_ref[pl.ds(base + 16 * pitch, 8, stride=pitch), :].astype(jnp.bfloat16)
        return jnp.concatenate([charge, charge], axis=1)

    def soft_of(begin):
        left = []
        right = []
        for side in range(2):
            operand_q = operand_of(plate_planes, plate_list[begin + side])
            blank = jnp.zeros_like(operand_q)
            left.append(operand_of(tower_planes, tower_list[begin + side]))
            pair = [operand_q, blank] if side == 0 else [blank, operand_q]
            right.append(jnp.concatenate(pair, axis=1))
        return lax.dot_general(
            jnp.concatenate(left, axis=0),
            jnp.concatenate(right, axis=0),
            (((0,), (0,)), ((), ())),
            preferred_element_type=jnp.float32,
        )

    def keep(soft, at):
        softs[at] = soft[:, : soft.shape[1] // 2]
        softs[at + 1] = soft[:, soft.shape[1] // 2 :]

    def consume(begin, ats):
        for at in ats:
            tower_base = tower_list[begin + at]
            plate_base = plate_list[begin + at]
            soft = jnp.maximum(softs[at], 0.0)
            square = soft * soft
            high = square.astype(jnp.bfloat16)
            low = (square - high.astype(jnp.float32)).astype(jnp.bfloat16)
            on_plate = jnp.dot(
                charge_of(tower_planes, tower_base),
                jnp.concatenate([high, low], axis=0),
                preferred_element_type=jnp.float32,
            )
            on_tower = lax.dot_general(
                charge_of(plate_planes, plate_base),
                jnp.concatenate([high, low], axis=1),
                (((1,), (1,)), ((), ())),
                preferred_element_type=jnp.float32,
            )
            tower_at = pl.ds(tower_base, 8, stride=pitch)
            plate_at = pl.ds(plate_base, 8, stride=pitch)
            tower_sums[tower_at, :] = tower_sums[tower_at, :] + on_tower
            plate_sums[plate_at, :] = plate_sums[plate_at, :] + on_plate

    def advance(step, unused):
        begin = step * group
        for at in range(0, group, 2):
            following = soft_of(begin + group + at)
            consume(begin, (at, at + 1))
            keep(following, at)
        return unused

    for at in range(0, group, 2):
        keep(soft_of(at), at)
    lax.fori_loop(0, lax.div(count + (group - 1), group), advance, 0)

    def tower_part(block):
        strength = strength_refs[block % rows_held][3]
        base = block * (planes * pitch)
        return apply_sums(tower_sums, base, tower_place(block), strength, clusters)

    def plate_part(line, rise):
        slot, above = plate_slot(line, rise)
        strength = strength_refs[rows_held + line % lines_held * heights + rise][3]
        base = slot * (planes * pitch)
        return apply_sums(plate_sums, base, plate_place(line, rise, above), strength, clusters)

    def add(first, second):
        return [one + two for one, two in zip(first, second)]

    forces = {}
    for block in range(towers):
        place = block % rows_held
        part = tower_part(block)
        forces[place] = add(forces[place], part) if place in forces else part
    for line in range(lines):
        for rise in range(heights):
            place = rows_held + line % lines_held * heights + rise
            part = plate_part(line, rise)
            forces[place] = add(forces[place], part) if place in forces else part
    forces[own_row] = add(forces[own_row], forces.pop(rows_held))
    for ref, place in zip(force_refs, sorted(forces)):
        for at in range(3):
            ref[at] = forces[place][at]


def pair_forces(height, count, tower_list, plate_list, places, strengths, held, sizes, order):
    rows_held, lines_held = held
    heights = sizes[2]
    clusters, size = places[0].shape[1:]
    blocks = len(places)
    towers = 2 * reach + 1
    kernel = functools.partial(
        pair_kernel,
        rows_held=rows_held,
        lines_held=lines_held,
        heights=heights,
        clusters=clusters,
        order=order,
    )
    smem = pl.BlockSpec(memory_space=pltpu.SMEM)
    vmem = pl.BlockSpec(memory_space=pltpu.VMEM)
    pairs = tower_list.shape[0]
    block_rows = planes * (clusters + 1)
    force = jax.ShapeDtypeStruct((3, clusters, size), jnp.float32)
    return pl.pallas_call(
        kernel,
        out_shape=(force,) * (blocks - 1),
        in_specs=[smem] * 4 + [vmem] * (2 * blocks),
        out_specs=(vmem,) * (blocks - 1),
        scratch_shapes=[
            pltpu.VMEM(((towers + 1) * block_rows, size), jnp.float32),
            pltpu.VMEM(((lines * heights + 1) * block_rows, size), jnp.float32),
            pltpu.VMEM(((towers + 1) * block_rows, size), jnp.float32),
            pltpu.VMEM(((lines * heights + 1) * block_rows, size), jnp.float32),
            pltpu.VMEM((group, size, size), jnp.float32),
        ],
        compiler_params=pltpu.CompilerParams(vmem_limit_bytes=grant),
        cost_estimate=pl.CostEstimate(
            flops=pairs * size * size * 40, bytes_accessed=1 << 20, transcendentals=0
        ),
    )(
        height,
        count,
        tower_list,
        plate_list,
        *[places[block] for block in order],
        *[strengths[block] for block in order],
    )


def shift_row(value, steps, count):
    return lax.ppermute(value, "gx", [(at, (at + steps) % count) for at in range(count)])


def shift_plane(value, line_steps, height_steps, line_count, height_count):
    pairs = [
        (
            at * height_count + up,
            (at + line_steps) % line_count * height_count + (up + height_steps) % height_count,
        )
        for at in range(line_count)
        for up in range(height_count)
    ]
    return lax.ppermute(value, ("gy", "gz"), pairs)


def plan(row_count, line_count, height_count):
    rows_held = min(row_count, 2 * reach + 1)
    lines_held = min(line_count, lines)
    rows = [(held - reach) % row_count for held in range(rows_held)]
    plates = [(line, rise) for line in range(lines_held) for rise in range(height_count)]
    return rows, plates, lines_held


def issue_order(rows, plates):
    far_rows = sorted((offset for offset in rows if offset != 0), reverse=True)
    near = sorted((place for place in plates if place != (0, 0)), key=lambda at: (-at[1], -at[0]))
    return far_rows + near


def collect(value, rows, plates, sizes):
    row_count, line_count, height_count = sizes
    got = {}
    for place in issue_order(rows, plates)[::-1]:
        if isinstance(place, tuple):
            line, rise = place
            got[place] = shift_plane(value, -line, -rise, line_count, height_count)
        else:
            got[place] = shift_row(value, -place, row_count)
    got[0] = got[(0, 0)] = value
    return [got[offset] for offset in rows] + [got[place] for place in plates]


def give_back(forces, rows, plates, sizes):
    row_count, line_count, height_count = sizes
    remote = dict(zip(list(rows) + [place for place in plates if place != (0, 0)], forces))
    total = remote.pop(0)
    moved = []
    for place in issue_order(rows, plates):
        part = remote[place]
        if isinstance(place, tuple):
            moved.append(shift_plane(part, *place, line_count, height_count))
        else:
            moved.append(shift_row(part, place, row_count))
    for part in moved:
        total = total + part
    return total


def bases_of(slots, count, clusters, blank_block):
    block_rows = planes * (clusters + 1)
    base = lax.div(slots, clusters) * block_rows + lax.rem(slots, clusters)
    live = lax.broadcasted_iota(jnp.int32, slots.shape, 0) < count
    base = jnp.where(live, base, blank_block * block_rows)
    return jnp.pad(base, (0, 2 * group), constant_values=blank_block * block_rows)


def shards(positions, velocities, strength, tower_slots, plate_slots, pair_count):
    coords = positions[0, 0, 0]
    speeds = velocities[0, 0, 0]
    tower_list = tower_slots[0, 0, 0]
    plate_list = plate_slots[0, 0, 0]
    count = pair_count.reshape(1)
    clusters = coords.shape[1]
    sizes = tuple(lax.axis_size(name) for name in ("gx", "gy", "gz"))
    tower_list = bases_of(tower_list, count[0], clusters, 2 * reach + 1)
    plate_list = bases_of(plate_list, count[0], clusters, lines * sizes[2])
    rows, plates, lines_held = plan(*sizes)
    height = lax.axis_index("gz").astype(jnp.int32).reshape(1)
    keys = list(rows) + list(plates)
    issued = issue_order(rows, plates)
    order = [keys.index(0), keys.index((0, 0))] + [keys.index(place) for place in issued[::-1]]
    packed = jnp.concatenate([coords, strength[0, 0]], axis=0)
    strengths = collect(packed, rows, plates, sizes)
    places = strengths
    for leap_index in range(2):
        if leap_index > 0:
            places = collect(coords, rows, plates, sizes)
        forces = pair_forces(
            height,
            count,
            tower_list,
            plate_list,
            places,
            strengths,
            (len(rows), lines_held),
            sizes,
            order,
        )
        force = give_back(forces, rows, plates, sizes)
        speeds = speeds + time_step * force
        coords = coords + time_step * speeds
    return (coords[None, None, None], speeds[None, None, None])


def solution(mesh):
    in_specs = (
        P("gx", "gy", "gz", None, None, None),
        P("gx", "gy", "gz", None, None, None),
        P("gx", "gy", "gz", None, None),
        P("gx", "gy", "gz", None),
        P("gx", "gy", "gz", None),
        P("gx", "gy", "gz"),
    )
    out_specs = (P("gx", "gy", "gz", None, None, None), P("gx", "gy", "gz", None, None, None))
    return jax.shard_map(shards, mesh=mesh, in_specs=in_specs, out_specs=out_specs, check_vma=False)
```

```python
import functools

import jax
import jax.numpy as jnp
from jax import lax
from jax.experimental import pallas as pl
from jax.experimental.pallas import tpu as pltpu
from jax.sharding import PartitionSpec as P

time_step = 0.02
repulsion = 4.0
reach = 2
lines = 3
group = 64
lead = 8
planes = 24
grant = 32 << 20


def split(value):
    high = value.astype(jnp.bfloat16).astype(jnp.float32)
    return high, value - high


def split_three(value):
    high, rest = split(value)
    middle, low = split(rest)
    return high, middle, low


def norm_of(place):
    return place[0] * place[0] + place[1] * place[1] + place[2] * place[2]


def write_planes(planes_ref, base, rows, clusters):
    for at, row in enumerate(rows):
        planes_ref[pl.ds(base + at * (clusters + 1), clusters), :] = row


def charges(place, strength):
    parts = [split(strength * value) for value in place] + [split(strength)]
    return [part[0] for part in parts] + [part[1] for part in parts]


def tower_rows(place, strength):
    ones = jnp.ones_like(strength)
    parts = [split(value) for value in place]
    high = [part[0] for part in parts]
    middle = [part[1] for part in parts]
    norm = split_three(-0.25 * norm_of(place))
    operand = high + [norm[0]] + high + [norm[1]] + middle + [norm[2], ones, ones, ones, 0.0 * ones]
    return operand + charges(place, strength)


def plate_rows(place, strength):
    ones = jnp.ones_like(strength)
    parts = [split(0.5 * value) for value in place]
    high = [part[0] for part in parts]
    middle = [part[1] for part in parts]
    norm = split_three(1.0 - 0.25 * norm_of(place))
    operand = high + [ones] + middle + [ones] + high + [ones] + list(norm) + [0.0 * ones]
    return operand + charges(place, strength)


def apply_sums(sums, base, place, strength, clusters):
    row = [sums[pl.ds(base + at * (clusters + 1), clusters), :] for at in range(8)]
    total = [row[at] + row[at + 4] for at in range(4)]
    scale = repulsion * strength
    return [scale * (place[at] * total[3] - total[at]) for at in range(3)]


def pair_kernel(*refs, rows_held, lines_held, heights, clusters, order):
    height_ref, count_ref, tower_list, plate_list = refs[:4]
    blocks = rows_held + lines_held * heights
    place_refs = [refs[4 + order.index(block)] for block in range(blocks)]
    strength_refs = [refs[4 + blocks + order.index(block)] for block in range(blocks)]
    force_refs = refs[4 + 2 * blocks : 4 + 3 * blocks - 1]
    tower_planes, plate_planes, tower_sums, plate_sums, softs = refs[4 + 3 * blocks - 1 :]
    count = count_ref[0]
    height = height_ref[0]
    own_row = reach % rows_held
    towers = 2 * reach + 1
    pitch = clusters + 1
    blank_rows = jnp.zeros((8, tower_planes.shape[1]), jnp.float32)

    def tower_place(block):
        ref = place_refs[block % rows_held]
        return [ref[0] + (block - reach - 0.5), ref[1] - 1.0, ref[2] - 0.5]

    def plate_slot(line, rise):
        level = height + rise
        level = jnp.where(level >= heights, level - heights, level)
        return line * heights + level, (level - height).astype(jnp.float32) - 0.5

    def plate_place(line, rise, above):
        ref = place_refs[rows_held + line % lines_held * heights + rise]
        return [ref[0] - 0.5, ref[1] + (line - 1.0), ref[2] + above]

    for block in range(towers):
        strength = strength_refs[block % rows_held][3]
        base = block * (planes * pitch)
        write_planes(tower_planes, base, tower_rows(tower_place(block), strength), clusters)
    for line in range(lines):
        for rise in range(heights):
            slot, above = plate_slot(line, rise)
            strength = strength_refs[rows_held + line % lines_held * heights + rise][3]
            base = slot * (planes * pitch)
            rows = plate_rows(plate_place(line, rise, above), strength)
            write_planes(plate_planes, base, rows, clusters)
    for ref, sums, blocks_here in (
        (tower_planes, tower_sums, towers),
        (plate_planes, plate_sums, lines * heights),
    ):
        for at in range(0, planes, 8):
            ref[pl.ds(blocks_here * planes * pitch + at * pitch, 8, stride=pitch), :] = blank_rows
        for block in range(blocks_here + 1):
            sums[pl.ds(block * planes * pitch, 8 * pitch), :] = jnp.zeros(
                (8 * pitch, sums.shape[1]), jnp.float32
            )

    def operand_of(planes_ref, base):
        lower = planes_ref[pl.ds(base, 8, stride=pitch), :]
        upper = planes_ref[pl.ds(base + 8 * pitch, 8, stride=pitch), :]
        return jnp.concatenate([lower, upper], axis=0).astype(jnp.bfloat16)

    def charge_of(planes_ref, base):
        charge = planes_ref[pl.ds(base + 16 * pitch, 8, stride=pitch), :].astype(jnp.bfloat16)
        return jnp.concatenate([charge, charge], axis=1)

    def soft_of(begin):
        left = []
        right = []
        for side in range(2):
            operand_q = operand_of(plate_planes, plate_list[begin + side])
            blank = jnp.zeros_like(operand_q)
            left.append(operand_of(tower_planes, tower_list[begin + side]))
            pair = [operand_q, blank] if side == 0 else [blank, operand_q]
            right.append(jnp.concatenate(pair, axis=1))
        return lax.dot_general(
            jnp.concatenate(left, axis=0),
            jnp.concatenate(right, axis=0),
            (((0,), (0,)), ((), ())),
            preferred_element_type=jnp.float32,
        )

    def keep(soft, at):
        softs[at] = soft[:, : soft.shape[1] // 2]
        softs[at + 1] = soft[:, soft.shape[1] // 2 :]

    def consume(begin, ats):
        for at in ats:
            tower_base = tower_list[begin + at]
            plate_base = plate_list[begin + at]
            soft = jnp.maximum(softs[at % lead], 0.0)
            square = soft * soft
            high = square.astype(jnp.bfloat16)
            low = (square - high.astype(jnp.float32)).astype(jnp.bfloat16)
            on_plate = jnp.dot(
                charge_of(tower_planes, tower_base),
                jnp.concatenate([high, low], axis=0),
                preferred_element_type=jnp.float32,
            )
            on_tower = lax.dot_general(
                jnp.concatenate([high, low], axis=1),
                charge_of(plate_planes, plate_base),
                (((1,), (1,)), ((), ())),
                preferred_element_type=jnp.float32,
            ).T
            tower_at = pl.ds(tower_base, 8, stride=pitch)
            plate_at = pl.ds(plate_base, 8, stride=pitch)
            tower_sums[tower_at, :] = tower_sums[tower_at, :] + on_tower
            plate_sums[plate_at, :] = plate_sums[plate_at, :] + on_plate

    def advance(step, unused):
        begin = step * group
        for at in range(0, group, 2):
            following = soft_of(begin + lead + at)
            consume(begin, (at, at + 1))
            keep(following, at % lead)
        return unused

    for at in range(0, lead, 2):
        keep(soft_of(at), at)
    lax.fori_loop(0, lax.div(count + (group - 1), group), advance, 0)

    def tower_part(block):
        strength = strength_refs[block % rows_held][3]
        base = block * (planes * pitch)
        return apply_sums(tower_sums, base, tower_place(block), strength, clusters)

    def plate_part(line, rise):
        slot, above = plate_slot(line, rise)
        strength = strength_refs[rows_held + line % lines_held * heights + rise][3]
        base = slot * (planes * pitch)
        return apply_sums(plate_sums, base, plate_place(line, rise, above), strength, clusters)

    def add(first, second):
        return [one + two for one, two in zip(first, second)]

    forces = {}
    for block in range(towers):
        place = block % rows_held
        part = tower_part(block)
        forces[place] = add(forces[place], part) if place in forces else part
    for line in range(lines):
        for rise in range(heights):
            place = rows_held + line % lines_held * heights + rise
            part = plate_part(line, rise)
            forces[place] = add(forces[place], part) if place in forces else part
    forces[own_row] = add(forces[own_row], forces.pop(rows_held))
    for ref, place in zip(force_refs, sorted(forces)):
        for at in range(3):
            ref[at] = forces[place][at]


def pair_forces(height, count, tower_list, plate_list, places, strengths, held, sizes, order):
    rows_held, lines_held = held
    heights = sizes[2]
    clusters, size = places[0].shape[1:]
    blocks = len(places)
    towers = 2 * reach + 1
    kernel = functools.partial(
        pair_kernel,
        rows_held=rows_held,
        lines_held=lines_held,
        heights=heights,
        clusters=clusters,
        order=order,
    )
    smem = pl.BlockSpec(memory_space=pltpu.SMEM)
    vmem = pl.BlockSpec(memory_space=pltpu.VMEM)
    pairs = tower_list.shape[0]
    block_rows = planes * (clusters + 1)
    force = jax.ShapeDtypeStruct((3, clusters, size), jnp.float32)
    return pl.pallas_call(
        kernel,
        out_shape=(force,) * (blocks - 1),
        in_specs=[smem] * 4 + [vmem] * (2 * blocks),
        out_specs=(vmem,) * (blocks - 1),
        scratch_shapes=[
            pltpu.VMEM(((towers + 1) * block_rows, size), jnp.float32),
            pltpu.VMEM(((lines * heights + 1) * block_rows, size), jnp.float32),
            pltpu.VMEM(((towers + 1) * block_rows, size), jnp.float32),
            pltpu.VMEM(((lines * heights + 1) * block_rows, size), jnp.float32),
            pltpu.VMEM((lead, size, size), jnp.float32),
        ],
        compiler_params=pltpu.CompilerParams(vmem_limit_bytes=grant),
        cost_estimate=pl.CostEstimate(
            flops=pairs * size * size * 40, bytes_accessed=1 << 20, transcendentals=0
        ),
    )(
        height,
        count,
        tower_list,
        plate_list,
        *[places[block] for block in order],
        *[strengths[block] for block in order],
    )


def shift_row(value, steps, count):
    return lax.ppermute(value, "gx", [(at, (at + steps) % count) for at in range(count)])


def shift_plane(value, line_steps, height_steps, line_count, height_count):
    pairs = [
        (
            at * height_count + up,
            (at + line_steps) % line_count * height_count + (up + height_steps) % height_count,
        )
        for at in range(line_count)
        for up in range(height_count)
    ]
    return lax.ppermute(value, ("gy", "gz"), pairs)


def plan(row_count, line_count, height_count):
    rows_held = min(row_count, 2 * reach + 1)
    lines_held = min(line_count, lines)
    rows = [(held - reach) % row_count for held in range(rows_held)]
    plates = [(line, rise) for line in range(lines_held) for rise in range(height_count)]
    return rows, plates, lines_held


def issue_order(rows, plates):
    far_rows = sorted((offset for offset in rows if offset != 0), reverse=True)
    near = sorted((place for place in plates if place != (0, 0)), key=lambda at: (-at[1], -at[0]))
    return far_rows + near


def collect(value, rows, plates, sizes):
    row_count, line_count, height_count = sizes
    got = {}
    for place in issue_order(rows, plates)[::-1]:
        if isinstance(place, tuple):
            line, rise = place
            got[place] = shift_plane(value, -line, -rise, line_count, height_count)
        else:
            got[place] = shift_row(value, -place, row_count)
    got[0] = got[(0, 0)] = value
    return [got[offset] for offset in rows] + [got[place] for place in plates]


def give_back(forces, rows, plates, sizes):
    row_count, line_count, height_count = sizes
    remote = dict(zip(list(rows) + [place for place in plates if place != (0, 0)], forces))
    total = remote.pop(0)
    moved = []
    for place in issue_order(rows, plates):
        part = remote[place]
        if isinstance(place, tuple):
            moved.append(shift_plane(part, *place, line_count, height_count))
        else:
            moved.append(shift_row(part, place, row_count))
    for part in moved:
        total = total + part
    return total


def bases_of(slots, count, clusters, blank_block):
    block_rows = planes * (clusters + 1)
    base = lax.div(slots, clusters) * block_rows + lax.rem(slots, clusters)
    live = lax.broadcasted_iota(jnp.int32, slots.shape, 0) < count
    base = jnp.where(live, base, blank_block * block_rows)
    return jnp.pad(base, (0, group + lead), constant_values=blank_block * block_rows)


def shards(positions, velocities, strength, tower_slots, plate_slots, pair_count):
    coords = positions[0, 0, 0]
    speeds = velocities[0, 0, 0]
    tower_list = tower_slots[0, 0, 0]
    plate_list = plate_slots[0, 0, 0]
    count = pair_count.reshape(1)
    clusters = coords.shape[1]
    sizes = tuple(lax.axis_size(name) for name in ("gx", "gy", "gz"))
    tower_list = bases_of(tower_list, count[0], clusters, 2 * reach + 1)
    plate_list = bases_of(plate_list, count[0], clusters, lines * sizes[2])
    rows, plates, lines_held = plan(*sizes)
    height = lax.axis_index("gz").astype(jnp.int32).reshape(1)
    keys = list(rows) + list(plates)
    issued = issue_order(rows, plates)
    order = [keys.index(0), keys.index((0, 0))] + [keys.index(place) for place in issued[::-1]]
    packed = jnp.concatenate([coords, strength[0, 0]], axis=0)
    strengths = collect(packed, rows, plates, sizes)
    places = strengths
    for leap_index in range(2):
        if leap_index > 0:
            places = collect(coords, rows, plates, sizes)
        forces = pair_forces(
            height,
            count,
            tower_list,
            plate_list,
            places,
            strengths,
            (len(rows), lines_held),
            sizes,
            order,
        )
        force = give_back(forces, rows, plates, sizes)
        speeds = speeds + time_step * force
        coords = coords + time_step * speeds
    return (coords[None, None, None], speeds[None, None, None])


def solution(mesh):
    in_specs = (
        P("gx", "gy", "gz", None, None, None),
        P("gx", "gy", "gz", None, None, None),
        P("gx", "gy", "gz", None, None),
        P("gx", "gy", "gz", None),
        P("gx", "gy", "gz", None),
        P("gx", "gy", "gz"),
    )
    out_specs = (P("gx", "gy", "gz", None, None, None), P("gx", "gy", "gz", None, None, None))
    return jax.shard_map(shards, mesh=mesh, in_specs=in_specs, out_specs=out_specs, check_vma=False)
```

```python
import functools

import jax
import jax.numpy as jnp
from jax import lax
from jax.experimental import pallas as pl
from jax.experimental.pallas import tpu as pltpu
from jax.sharding import PartitionSpec as P


time_step = 0.02
repulsion = 4.0
reach = 2
lines = 3
group = 64
lead = 8
planes = 24
grant = 32 << 20


def split(value):
    high = value.astype(jnp.bfloat16).astype(jnp.float32)
    return high, value - high


def split_three(value):
    high, rest = split(value)
    middle, low = split(rest)
    return high, middle, low


def norm_of(place):
    return place[0] * place[0] + place[1] * place[1] + place[2] * place[2]


def write_planes(planes_ref, base, rows, clusters):
    for at, row in enumerate(rows):
        planes_ref[pl.ds(base + at * (clusters + 1), clusters), :] = row


def charges(place, strength):
    parts = [split(strength * value) for value in place] + [split(strength)]
    return [part[0] for part in parts] + [part[1] for part in parts]


def tower_rows(place, strength):
    ones = jnp.ones_like(strength)
    parts = [split(value) for value in place]
    high = [part[0] for part in parts]
    middle = [part[1] for part in parts]
    norm = split_three(-0.25 * norm_of(place))
    operand = high + [norm[0]] + high + [norm[1]] + middle + [norm[2], ones, ones, ones, 0.0 * ones]
    return operand + charges(place, strength)


def plate_rows(place, strength):
    ones = jnp.ones_like(strength)
    parts = [split(0.5 * value) for value in place]
    high = [part[0] for part in parts]
    middle = [part[1] for part in parts]
    norm = split_three(1.0 - 0.25 * norm_of(place))
    operand = high + [ones] + middle + [ones] + high + [ones] + list(norm) + [0.0 * ones]
    return operand + charges(place, strength)


def apply_sums(sums, base, place, strength, clusters):
    row = [sums[pl.ds(base + at * (clusters + 1), clusters), :] for at in range(8)]
    total = [row[at] + row[at + 4] for at in range(4)]
    scale = repulsion * strength
    return [scale * (place[at] * total[3] - total[at]) for at in range(3)]


def views(refs, where):
    return [
        refs[operand] if part is None else refs[operand].at[part] for operand, part in where
    ]


def pair_kernel(*refs, rows_held, lines_held, heights, clusters, where_place, where_strength):
    height_ref, count_ref, tower_list, plate_list = refs[:4]
    place_count = 1 + max(operand for operand, part in where_place)
    strength_count = 1 + max(operand for operand, part in where_strength)
    place_refs = views(refs[4 : 4 + place_count], where_place)
    strength_refs = views(refs[4 + place_count : 4 + place_count + strength_count], where_strength)
    force_refs = refs[4 + place_count + strength_count : -5]
    tower_planes, plate_planes, tower_sums, plate_sums, softs = refs[-5:]
    count = count_ref[0]
    height = height_ref[0]
    own_row = reach % rows_held
    towers = 2 * reach + 1
    pitch = clusters + 1
    blank_rows = jnp.zeros((8, tower_planes.shape[1]), jnp.float32)

    def tower_place(block):
        ref = place_refs[block % rows_held]
        return [ref[0] + (block - reach - 0.5), ref[1] - 1.0, ref[2] - 0.5]

    def plate_slot(line, rise):
        level = height + rise
        level = jnp.where(level >= heights, level - heights, level)
        return line * heights + level, (level - height).astype(jnp.float32) - 0.5

    def plate_place(line, rise, above):
        ref = place_refs[rows_held + line % lines_held * heights + rise]
        return [ref[0] - 0.5, ref[1] + (line - 1.0), ref[2] + above]

    for block in range(towers):
        strength = strength_refs[block % rows_held][3]
        base = block * (planes * pitch)
        write_planes(tower_planes, base, tower_rows(tower_place(block), strength), clusters)
    for line in range(lines):
        for rise in range(heights):
            slot, above = plate_slot(line, rise)
            strength = strength_refs[rows_held + line % lines_held * heights + rise][3]
            base = slot * (planes * pitch)
            rows = plate_rows(plate_place(line, rise, above), strength)
            write_planes(plate_planes, base, rows, clusters)
    for ref, sums, blocks_here in (
        (tower_planes, tower_sums, towers),
        (plate_planes, plate_sums, lines * heights),
    ):
        for at in range(0, planes, 8):
            ref[pl.ds(blocks_here * planes * pitch + at * pitch, 8, stride=pitch), :] = blank_rows
        for block in range(blocks_here + 1):
            sums[pl.ds(block * planes * pitch, 8 * pitch), :] = jnp.zeros(
                (8 * pitch, sums.shape[1]), jnp.float32
            )

    def operand_of(planes_ref, base):
        lower = planes_ref[pl.ds(base, 8, stride=pitch), :]
        upper = planes_ref[pl.ds(base + 8 * pitch, 8, stride=pitch), :]
        return jnp.concatenate([lower, upper], axis=0).astype(jnp.bfloat16)

    def charge_of(planes_ref, base):
        charge = planes_ref[pl.ds(base + 16 * pitch, 8, stride=pitch), :].astype(jnp.bfloat16)
        return jnp.concatenate([charge, charge], axis=1)

    def soft_of(begin):
        left = []
        right = []
        for side in range(2):
            operand_q = operand_of(plate_planes, plate_list[begin + side])
            blank = jnp.zeros_like(operand_q)
            left.append(operand_of(tower_planes, tower_list[begin + side]))
            pair = [operand_q, blank] if side == 0 else [blank, operand_q]
            right.append(jnp.concatenate(pair, axis=1))
        return lax.dot_general(
            jnp.concatenate(left, axis=0),
            jnp.concatenate(right, axis=0),
            (((0,), (0,)), ((), ())),
            preferred_element_type=jnp.float32,
        )

    def keep(soft, at):
        softs[at] = soft[:, : soft.shape[1] // 2]
        softs[at + 1] = soft[:, soft.shape[1] // 2 :]

    def consume(begin, ats):
        for at in ats:
            tower_base = tower_list[begin + at]
            plate_base = plate_list[begin + at]
            soft = jnp.maximum(softs[at % lead], 0.0)
            square = soft * soft
            high = square.astype(jnp.bfloat16)
            low = (square - high.astype(jnp.float32)).astype(jnp.bfloat16)
            on_plate = jnp.dot(
                charge_of(tower_planes, tower_base),
                jnp.concatenate([high, low], axis=0),
                preferred_element_type=jnp.float32,
            )
            on_tower = lax.dot_general(
                jnp.concatenate([high, low], axis=1),
                charge_of(plate_planes, plate_base),
                (((1,), (1,)), ((), ())),
                preferred_element_type=jnp.float32,
            ).T
            tower_at = pl.ds(tower_base, 8, stride=pitch)
            plate_at = pl.ds(plate_base, 8, stride=pitch)
            tower_sums[tower_at, :] = tower_sums[tower_at, :] + on_tower
            plate_sums[plate_at, :] = plate_sums[plate_at, :] + on_plate

    def advance(step, unused):
        begin = step * group
        for at in range(0, group, 2):
            following = soft_of(begin + lead + at)
            consume(begin, (at, at + 1))
            keep(following, at % lead)
        return unused

    for at in range(0, lead, 2):
        keep(soft_of(at), at)
    lax.fori_loop(0, lax.div(count + (group - 1), group), advance, 0)

    def tower_part(block):
        strength = strength_refs[block % rows_held][3]
        base = block * (planes * pitch)
        return apply_sums(tower_sums, base, tower_place(block), strength, clusters)

    def plate_part(line, rise):
        slot, above = plate_slot(line, rise)
        strength = strength_refs[rows_held + line % lines_held * heights + rise][3]
        base = slot * (planes * pitch)
        return apply_sums(plate_sums, base, plate_place(line, rise, above), strength, clusters)

    def add(first, second):
        return [one + two for one, two in zip(first, second)]

    forces = {}
    for block in range(towers):
        place = block % rows_held
        part = tower_part(block)
        forces[place] = add(forces[place], part) if place in forces else part
    for line in range(lines):
        for rise in range(heights):
            place = rows_held + line % lines_held * heights + rise
            part = plate_part(line, rise)
            forces[place] = add(forces[place], part) if place in forces else part
    forces[own_row] = add(forces[own_row], forces.pop(rows_held))
    targets = [(ref, held) for held, ref in enumerate(force_refs[:rows_held])]
    for line in range(1, lines_held):
        targets.append((force_refs[rows_held + line - 1], rows_held + line * heights))
    for rise in range(1, heights):
        ref = force_refs[rows_held + lines_held - 2 + rise]
        for line in range(lines_held):
            targets.append((ref.at[line], rows_held + line * heights + rise))
    for ref, held in targets:
        for at in range(3):
            ref[at] = forces[held][at]


def pair_forces(height, count, tower_list, plate_list, places, strengths, held, heights):
    rows_held, lines_held = held
    place_operands, where_place = places
    strength_operands, where_strength = strengths
    clusters, size = place_operands[0].shape[1:]
    towers = 2 * reach + 1
    kernel = functools.partial(
        pair_kernel,
        rows_held=rows_held,
        lines_held=lines_held,
        heights=heights,
        clusters=clusters,
        where_place=where_place,
        where_strength=where_strength,
    )
    smem = pl.BlockSpec(memory_space=pltpu.SMEM)
    vmem = pl.BlockSpec(memory_space=pltpu.VMEM)
    pairs = tower_list.shape[0]
    block_rows = planes * (clusters + 1)
    force = jax.ShapeDtypeStruct((3, clusters, size), jnp.float32)
    raised = jax.ShapeDtypeStruct((lines_held, 3, clusters, size), jnp.float32)
    out_shape = (force,) * (rows_held + lines_held - 1) + (raised,) * (heights - 1)
    return pl.pallas_call(
        kernel,
        out_shape=out_shape,
        in_specs=[smem] * 4 + [vmem] * (len(place_operands) + len(strength_operands)),
        out_specs=(vmem,) * len(out_shape),
        scratch_shapes=[
            pltpu.VMEM(((towers + 1) * block_rows, size), jnp.float32),
            pltpu.VMEM(((lines * heights + 1) * block_rows, size), jnp.float32),
            pltpu.VMEM(((towers + 1) * block_rows, size), jnp.float32),
            pltpu.VMEM(((lines * heights + 1) * block_rows, size), jnp.float32),
            pltpu.VMEM((lead, size, size), jnp.float32),
        ],
        compiler_params=pltpu.CompilerParams(vmem_limit_bytes=grant),
        cost_estimate=pl.CostEstimate(
            flops=pairs * size * size * 40, bytes_accessed=1 << 20, transcendentals=0
        ),
    )(height, count, tower_list, plate_list, *place_operands, *strength_operands)


def shift_row(value, steps, count):
    return lax.ppermute(value, "gx", [(at, (at + steps) % count) for at in range(count)])


def shift_plane(value, line_steps, height_steps, line_count, height_count):
    pairs = [
        (
            at * height_count + up,
            (at + line_steps) % line_count * height_count + (up + height_steps) % height_count,
        )
        for at in range(line_count)
        for up in range(height_count)
    ]
    return lax.ppermute(value, ("gy", "gz"), pairs)


def plan(row_count, line_count, height_count):
    rows_held = min(row_count, 2 * reach + 1)
    lines_held = min(line_count, lines)
    rows = [(held - reach) % row_count for held in range(rows_held)]
    plates = [(line, rise) for line in range(lines_held) for rise in range(height_count)]
    return rows, plates, lines_held


def issue_order(rows, plates):
    far_rows = sorted((offset for offset in rows if offset != 0), reverse=True)
    near = sorted((place for place in plates if place != (0, 0)), key=lambda at: (-at[1], -at[0]))
    return far_rows + near


def collect(value, rows, plates, sizes):
    row_count, line_count, height_count = sizes
    got = {}
    issued = issue_order(rows, plates)[::-1]
    for place in issued:
        if isinstance(place, tuple):
            line, rise = place
            got[place] = shift_plane(value, -line, -rise, line_count, height_count)
        else:
            got[place] = shift_row(value, -place, row_count)
    got[0] = value
    operands = [0] + issued
    where = [(operands.index(key), None) for key in rows]
    where += [(operands.index(key if key != (0, 0) else 0), None) for key in plates]
    return [got[key] for key in operands], tuple(where)


def far_rows(rows):
    return sorted((offset for offset in rows if offset != 0), reverse=True)


def collect_again(value, rows, lines_held, sizes):
    row_count, line_count, height_count = sizes
    operands = [value]
    where_line = [0]
    for line in range(lines_held - 1, 0, -1):
        operands.append(shift_plane(value, -line, 0, line_count, height_count))
    where_line += list(range(lines_held - 1, 0, -1))
    where_row = {0: 0}
    for offset in far_rows(rows):
        operands.append(shift_row(value, -offset, row_count))
        where_row[offset] = len(operands) - 1
    column = jnp.stack([operands[at] for at in where_line])
    where_rise = {}
    for rise in range(1, height_count):
        operands.append(shift_plane(column, 0, -rise, line_count, height_count))
        where_rise[rise] = len(operands) - 1
    where = [(where_row[offset], None) for offset in rows]
    for line in range(lines_held):
        where.append((where_line[line], None))
        where += [(where_rise[rise], line) for rise in range(1, height_count)]
    return operands, tuple(where)


def give_back(forces, rows, lines_held, sizes):
    row_count, line_count, height_count = sizes
    remote = dict(zip(rows, forces))
    total = remote.pop(0)
    own_lines = list(forces[len(rows) : len(rows) + lines_held - 1])
    raised = forces[len(rows) + lines_held - 1 :]
    moved = []
    for rise in range(1, height_count):
        moved.append(shift_plane(raised[rise - 1], 0, rise, line_count, height_count))
    for part in moved:
        own_lines = [own + part[at + 1] for at, own in enumerate(own_lines)]
        total = total + part[0]
    came = []
    for offset in far_rows(rows):
        came.append(shift_row(remote[offset], offset, row_count))
    for line in range(lines_held - 1, 0, -1):
        came.append(shift_plane(own_lines[line - 1], line, 0, line_count, height_count))
    for part in came:
        total = total + part
    return total


def bases_of(slots, count, clusters, blank_block):
    block_rows = planes * (clusters + 1)
    base = lax.div(slots, clusters) * block_rows + lax.rem(slots, clusters)
    live = lax.broadcasted_iota(jnp.int32, slots.shape, 0) < count
    base = jnp.where(live, base, blank_block * block_rows)
    return jnp.pad(base, (0, group + lead), constant_values=blank_block * block_rows)


def shards(positions, velocities, strength, tower_slots, plate_slots, pair_count):
    coords = positions[0, 0, 0]
    speeds = velocities[0, 0, 0]
    tower_list = tower_slots[0, 0, 0]
    plate_list = plate_slots[0, 0, 0]
    count = pair_count.reshape(1)
    clusters = coords.shape[1]
    sizes = tuple(lax.axis_size(name) for name in ("gx", "gy", "gz"))
    tower_list = bases_of(tower_list, count[0], clusters, 2 * reach + 1)
    plate_list = bases_of(plate_list, count[0], clusters, lines * sizes[2])
    rows, plates, lines_held = plan(*sizes)
    height = lax.axis_index("gz").astype(jnp.int32).reshape(1)
    packed = jnp.concatenate([coords, strength[0, 0]], axis=0)
    strengths = collect(packed, rows, plates, sizes)
    places = strengths
    for leap_index in range(2):
        if leap_index > 0:
            places = collect_again(coords, rows, lines_held, sizes)
        forces = pair_forces(
            height,
            count,
            tower_list,
            plate_list,
            places,
            strengths,
            (len(rows), lines_held),
            sizes[2],
        )
        force = give_back(forces, rows, lines_held, sizes)
        speeds = speeds + time_step * force
        coords = coords + time_step * speeds
    return (coords[None, None, None], speeds[None, None, None])


def solution(mesh):
    in_specs = (
        P("gx", "gy", "gz", None, None, None),
        P("gx", "gy", "gz", None, None, None),
        P("gx", "gy", "gz", None, None),
        P("gx", "gy", "gz", None),
        P("gx", "gy", "gz", None),
        P("gx", "gy", "gz"),
    )
    out_specs = (P("gx", "gy", "gz", None, None, None), P("gx", "gy", "gz", None, None, None))
    return jax.shard_map(
        shards, mesh=mesh, in_specs=in_specs, out_specs=out_specs, check_vma=False
    )
```

```python
import functools

import jax
import jax.numpy as jnp
from jax import lax
from jax.experimental import pallas as pl
from jax.experimental.pallas import tpu as pltpu
from jax.sharding import PartitionSpec as P


time_step = 0.02
repulsion = 4.0
reach = 2
lines = 3
group = 128
lead = 8
planes = 24
grant = 32 << 20


def split(value):
    high = value.astype(jnp.bfloat16).astype(jnp.float32)
    return high, value - high


def split_three(value):
    high, rest = split(value)
    middle, low = split(rest)
    return high, middle, low


def norm_of(place):
    return place[0] * place[0] + place[1] * place[1] + place[2] * place[2]


def write_planes(planes_ref, base, rows, clusters):
    for at, row in enumerate(rows):
        planes_ref[pl.ds(base + at * (clusters + 1), clusters), :] = row


def charges(place, strength):
    parts = [split(strength * value) for value in place] + [split(strength)]
    return [part[0] for part in parts] + [part[1] for part in parts]


def tower_rows(place, strength):
    ones = jnp.ones_like(strength)
    parts = [split(value) for value in place]
    high = [part[0] for part in parts]
    middle = [part[1] for part in parts]
    norm = split_three(-0.25 * norm_of(place))
    operand = high + [norm[0]] + high + [norm[1]] + middle + [norm[2], ones, ones, ones, 0.0 * ones]
    return operand + charges(place, strength)


def plate_rows(place, strength):
    ones = jnp.ones_like(strength)
    parts = [split(0.5 * value) for value in place]
    high = [part[0] for part in parts]
    middle = [part[1] for part in parts]
    norm = split_three(1.0 - 0.25 * norm_of(place))
    operand = high + [ones] + middle + [ones] + high + [ones] + list(norm) + [0.0 * ones]
    return operand + charges(place, strength)


def apply_sums(sums, base, place, strength, clusters):
    row = [sums[pl.ds(base + at * (clusters + 1), clusters), :] for at in range(8)]
    total = [row[at] + row[at + 4] for at in range(4)]
    scale = repulsion * strength
    return [scale * (place[at] * total[3] - total[at]) for at in range(3)]


def views(refs, where):
    return [
        refs[operand] if part is None else refs[operand].at[part] for operand, part in where
    ]


def pair_kernel(*refs, rows_held, lines_held, heights, clusters, where_place, where_strength):
    height_ref, count_ref, tower_list, plate_list = refs[:4]
    place_count = 1 + max(operand for operand, part in where_place)
    strength_count = 1 + max(operand for operand, part in where_strength)
    place_refs = views(refs[4 : 4 + place_count], where_place)
    strength_refs = views(refs[4 + place_count : 4 + place_count + strength_count], where_strength)
    force_refs = refs[4 + place_count + strength_count : -5]
    tower_planes, plate_planes, tower_sums, plate_sums, softs = refs[-5:]
    count = count_ref[0]
    height = height_ref[0]
    own_row = reach % rows_held
    towers = 2 * reach + 1
    pitch = clusters + 1
    blank_rows = jnp.zeros((8, tower_planes.shape[1]), jnp.float32)

    def tower_place(block):
        ref = place_refs[block % rows_held]
        return [ref[0] + (block - reach - 0.5), ref[1] - 1.0, ref[2] - 0.5]

    def plate_slot(line, rise):
        level = height + rise
        level = jnp.where(level >= heights, level - heights, level)
        return line * heights + level, (level - height).astype(jnp.float32) - 0.5

    def plate_place(line, rise, above):
        ref = place_refs[rows_held + line % lines_held * heights + rise]
        return [ref[0] - 0.5, ref[1] + (line - 1.0), ref[2] + above]

    for block in range(towers):
        strength = strength_refs[block % rows_held][3]
        base = block * (planes * pitch)
        write_planes(tower_planes, base, tower_rows(tower_place(block), strength), clusters)
    for line in range(lines):
        for rise in range(heights):
            slot, above = plate_slot(line, rise)
            strength = strength_refs[rows_held + line % lines_held * heights + rise][3]
            base = slot * (planes * pitch)
            rows = plate_rows(plate_place(line, rise, above), strength)
            write_planes(plate_planes, base, rows, clusters)
    for ref, sums, blocks_here in (
        (tower_planes, tower_sums, towers),
        (plate_planes, plate_sums, lines * heights),
    ):
        for at in range(0, planes, 8):
            ref[pl.ds(blocks_here * planes * pitch + at * pitch, 8, stride=pitch), :] = blank_rows
        for block in range(blocks_here + 1):
            sums[pl.ds(block * planes * pitch, 8 * pitch), :] = jnp.zeros(
                (8 * pitch, sums.shape[1]), jnp.float32
            )

    def operand_of(planes_ref, base):
        lower = planes_ref[pl.ds(base, 8, stride=pitch), :]
        upper = planes_ref[pl.ds(base + 8 * pitch, 8, stride=pitch), :]
        return jnp.concatenate([lower, upper], axis=0).astype(jnp.bfloat16)

    def charge_of(planes_ref, base):
        charge = planes_ref[pl.ds(base + 16 * pitch, 8, stride=pitch), :].astype(jnp.bfloat16)
        return jnp.concatenate([charge, charge], axis=1)

    def soft_of(begin):
        left = []
        right = []
        for side in range(2):
            operand_q = operand_of(plate_planes, plate_list[begin + side])
            blank = jnp.zeros_like(operand_q)
            left.append(operand_of(tower_planes, tower_list[begin + side]))
            pair = [operand_q, blank] if side == 0 else [blank, operand_q]
            right.append(jnp.concatenate(pair, axis=1))
        return lax.dot_general(
            jnp.concatenate(left, axis=0),
            jnp.concatenate(right, axis=0),
            (((0,), (0,)), ((), ())),
            preferred_element_type=jnp.float32,
        )

    def keep(soft, at):
        softs[at] = soft[:, : soft.shape[1] // 2]
        softs[at + 1] = soft[:, soft.shape[1] // 2 :]

    def consume(begin, ats):
        for at in ats:
            tower_base = tower_list[begin + at]
            plate_base = plate_list[begin + at]
            soft = jnp.maximum(softs[at % lead], 0.0)
            square = soft * soft
            high = square.astype(jnp.bfloat16)
            low = (square - high.astype(jnp.float32)).astype(jnp.bfloat16)
            on_plate = jnp.dot(
                charge_of(tower_planes, tower_base),
                jnp.concatenate([high, low], axis=0),
                preferred_element_type=jnp.float32,
            )
            on_tower = lax.dot_general(
                jnp.concatenate([high, low], axis=1),
                charge_of(plate_planes, plate_base),
                (((1,), (1,)), ((), ())),
                preferred_element_type=jnp.float32,
            ).T
            tower_at = pl.ds(tower_base, 8, stride=pitch)
            plate_at = pl.ds(plate_base, 8, stride=pitch)
            tower_sums[tower_at, :] = tower_sums[tower_at, :] + on_tower
            plate_sums[plate_at, :] = plate_sums[plate_at, :] + on_plate

    def advance(step, unused):
        begin = step * group
        for at in range(0, group, 2):
            following = soft_of(begin + lead + at)
            consume(begin, (at, at + 1))
            keep(following, at % lead)
        return unused

    for at in range(0, lead, 2):
        keep(soft_of(at), at)
    lax.fori_loop(0, lax.div(count + (group - 1), group), advance, 0)

    def tower_part(block):
        strength = strength_refs[block % rows_held][3]
        base = block * (planes * pitch)
        return apply_sums(tower_sums, base, tower_place(block), strength, clusters)

    def plate_part(line, rise):
        slot, above = plate_slot(line, rise)
        strength = strength_refs[rows_held + line % lines_held * heights + rise][3]
        base = slot * (planes * pitch)
        return apply_sums(plate_sums, base, plate_place(line, rise, above), strength, clusters)

    def add(first, second):
        return [one + two for one, two in zip(first, second)]

    forces = {}
    for block in range(towers):
        place = block % rows_held
        part = tower_part(block)
        forces[place] = add(forces[place], part) if place in forces else part
    for line in range(lines):
        for rise in range(heights):
            place = rows_held + line % lines_held * heights + rise
            part = plate_part(line, rise)
            forces[place] = add(forces[place], part) if place in forces else part
    forces[own_row] = add(forces[own_row], forces.pop(rows_held))
    targets = [(ref, held) for held, ref in enumerate(force_refs[:rows_held])]
    for line in range(1, lines_held):
        targets.append((force_refs[rows_held + line - 1], rows_held + line * heights))
    for rise in range(1, heights):
        ref = force_refs[rows_held + lines_held - 2 + rise]
        for line in range(lines_held):
            targets.append((ref.at[line], rows_held + line * heights + rise))
    for ref, held in targets:
        for at in range(3):
            ref[at] = forces[held][at]


def pair_forces(height, count, tower_list, plate_list, places, strengths, held, heights):
    rows_held, lines_held = held
    place_operands, where_place = places
    strength_operands, where_strength = strengths
    clusters, size = place_operands[0].shape[1:]
    towers = 2 * reach + 1
    kernel = functools.partial(
        pair_kernel,
        rows_held=rows_held,
        lines_held=lines_held,
        heights=heights,
        clusters=clusters,
        where_place=where_place,
        where_strength=where_strength,
    )
    smem = pl.BlockSpec(memory_space=pltpu.SMEM)
    vmem = pl.BlockSpec(memory_space=pltpu.VMEM)
    pairs = tower_list.shape[0]
    block_rows = planes * (clusters + 1)
    force = jax.ShapeDtypeStruct((3, clusters, size), jnp.float32)
    raised = jax.ShapeDtypeStruct((lines_held, 3, clusters, size), jnp.float32)
    out_shape = (force,) * (rows_held + lines_held - 1) + (raised,) * (heights - 1)
    return pl.pallas_call(
        kernel,
        out_shape=out_shape,
        in_specs=[smem] * 4 + [vmem] * (len(place_operands) + len(strength_operands)),
        out_specs=(vmem,) * len(out_shape),
        scratch_shapes=[
            pltpu.VMEM(((towers + 1) * block_rows, size), jnp.float32),
            pltpu.VMEM(((lines * heights + 1) * block_rows, size), jnp.float32),
            pltpu.VMEM(((towers + 1) * block_rows, size), jnp.float32),
            pltpu.VMEM(((lines * heights + 1) * block_rows, size), jnp.float32),
            pltpu.VMEM((lead, size, size), jnp.float32),
        ],
        compiler_params=pltpu.CompilerParams(vmem_limit_bytes=grant),
        cost_estimate=pl.CostEstimate(
            flops=pairs * size * size * 40, bytes_accessed=1 << 20, transcendentals=0
        ),
    )(height, count, tower_list, plate_list, *place_operands, *strength_operands)


def shift_row(value, steps, count):
    return lax.ppermute(value, "gx", [(at, (at + steps) % count) for at in range(count)])


def shift_plane(value, line_steps, height_steps, line_count, height_count):
    pairs = [
        (
            at * height_count + up,
            (at + line_steps) % line_count * height_count + (up + height_steps) % height_count,
        )
        for at in range(line_count)
        for up in range(height_count)
    ]
    return lax.ppermute(value, ("gy", "gz"), pairs)


def swap_row(value, mask, count):
    return lax.ppermute(value, "gx", [(at, at ^ mask) for at in range(count)])


def swappable(rows, row_count):
    return row_count in (2, 4) and len(rows) == row_count


def by_offset(swapped):
    odd = lax.axis_index("gx") % 2 == 1
    if 3 not in swapped:
        return dict(swapped)
    return {
        1: jnp.where(odd, swapped[3], swapped[1]),
        2: swapped[2],
        3: jnp.where(odd, swapped[1], swapped[3]),
    }


def fetch_row(value, offset, rows, row_count):
    if swappable(rows, row_count):
        return swap_row(value, offset, row_count)
    return shift_row(value, -offset, row_count)


def plan(row_count, line_count, height_count):
    rows_held = min(row_count, 2 * reach + 1)
    lines_held = min(line_count, lines)
    rows = [(held - reach) % row_count for held in range(rows_held)]
    plates = [(line, rise) for line in range(lines_held) for rise in range(height_count)]
    return rows, plates, lines_held


def first_order(rows, plates):
    away = far_rows(rows)
    near = sorted((place for place in plates if place != (0, 0)), key=lambda at: (-at[1], -at[0]))
    diagonal = [place for place in near if place[0] and place[1]]
    straight = [place for place in near if not (place[0] and place[1])]
    return away[:-1] + diagonal + away[-1:] + straight


def collect(value, rows, plates, sizes):
    row_count, line_count, height_count = sizes
    got = {}
    issued = first_order(rows, plates)[::-1]
    for place in issued:
        if isinstance(place, tuple):
            line, rise = place
            got[place] = shift_plane(value, -line, -rise, line_count, height_count)
        else:
            got[place] = fetch_row(value, place, rows, row_count)
    if swappable(rows, row_count):
        got.update(by_offset({place: got[place] for place in far_rows(rows)}))
    got[0] = value
    operands = [0] + issued
    where = [(operands.index(key), None) for key in rows]
    where += [(operands.index(key if key != (0, 0) else 0), None) for key in plates]
    return [got[key] for key in operands], tuple(where)


def far_rows(rows):
    return sorted((offset for offset in rows if offset != 0), reverse=True)


def collect_again(value, rows, lines_held, sizes):
    row_count, line_count, height_count = sizes
    got_lines = {0: value}
    for line in range(lines_held - 1, 0, -1):
        got_lines[line] = shift_plane(value, -line, 0, line_count, height_count)
    got_rows = {}
    for offset in far_rows(rows):
        got_rows[offset] = fetch_row(value, offset, rows, row_count)
    if swappable(rows, row_count):
        got_rows = by_offset(got_rows)
    column = jnp.stack([got_lines[line] for line in range(lines_held)])
    operands = [value]
    where_line = {0: 0}
    where_row = {0: 0}
    where_rise = {}
    for line in range(lines_held - 1, 0, -1):
        operands.append(got_lines[line])
        where_line[line] = len(operands) - 1
    for offset in far_rows(rows):
        operands.append(got_rows[offset])
        where_row[offset] = len(operands) - 1
    for rise in range(1, height_count):
        operands.append(shift_plane(column, 0, -rise, line_count, height_count))
        where_rise[rise] = len(operands) - 1
    where = [(where_row[offset], None) for offset in rows]
    for line in range(lines_held):
        where.append((where_line[line], None))
        where += [(where_rise[rise], line) for rise in range(1, height_count)]
    return operands, tuple(where)


def give_back(forces, rows, lines_held, sizes):
    row_count, line_count, height_count = sizes
    remote = dict(zip(rows, forces))
    total = remote.pop(0)
    own_lines = list(forces[len(rows) : len(rows) + lines_held - 1])
    raised = forces[len(rows) + lines_held - 1 :]
    moved = []
    for rise in range(1, height_count):
        moved.append(shift_plane(raised[rise - 1], 0, rise, line_count, height_count))
    for part in moved:
        own_lines = [own + part[at + 1] for at, own in enumerate(own_lines)]
        total = total + part[0]
    came = []
    for offset in far_rows(rows):
        came.append(shift_row(remote[offset], offset, row_count))
    for line in range(lines_held - 1, 0, -1):
        came.append(shift_plane(own_lines[line - 1], line, 0, line_count, height_count))
    for part in came:
        total = total + part
    return total


def bases_of(slots, count, clusters, blank_block):
    block_rows = planes * (clusters + 1)
    base = lax.div(slots, clusters) * block_rows + lax.rem(slots, clusters)
    live = lax.broadcasted_iota(jnp.int32, slots.shape, 0) < count
    base = jnp.where(live, base, blank_block * block_rows)
    return jnp.pad(base, (0, group + lead), constant_values=blank_block * block_rows)


def shards(positions, velocities, strength, tower_slots, plate_slots, pair_count):
    coords = positions[0, 0, 0]
    speeds = velocities[0, 0, 0]
    tower_list = tower_slots[0, 0, 0]
    plate_list = plate_slots[0, 0, 0]
    count = pair_count.reshape(1)
    clusters = coords.shape[1]
    sizes = tuple(lax.axis_size(name) for name in ("gx", "gy", "gz"))
    tower_list = bases_of(tower_list, count[0], clusters, 2 * reach + 1)
    plate_list = bases_of(plate_list, count[0], clusters, lines * sizes[2])
    rows, plates, lines_held = plan(*sizes)
    height = lax.axis_index("gz").astype(jnp.int32).reshape(1)
    packed = jnp.concatenate([coords, strength[0, 0]], axis=0)
    strengths = collect(packed, rows, plates, sizes)
    places = strengths
    for leap_index in range(2):
        if leap_index > 0:
            places = collect_again(coords, rows, lines_held, sizes)
        forces = pair_forces(
            height,
            count,
            tower_list,
            plate_list,
            places,
            strengths,
            (len(rows), lines_held),
            sizes[2],
        )
        force = give_back(forces, rows, lines_held, sizes)
        speeds = speeds + time_step * force
        coords = coords + time_step * speeds
    return (coords[None, None, None], speeds[None, None, None])


def solution(mesh):
    in_specs = (
        P("gx", "gy", "gz", None, None, None),
        P("gx", "gy", "gz", None, None, None),
        P("gx", "gy", "gz", None, None),
        P("gx", "gy", "gz", None),
        P("gx", "gy", "gz", None),
        P("gx", "gy", "gz"),
    )
    out_specs = (P("gx", "gy", "gz", None, None, None), P("gx", "gy", "gz", None, None, None))
    return jax.shard_map(
        shards, mesh=mesh, in_specs=in_specs, out_specs=out_specs, check_vma=False
    )
```
